128 devices in a mesh: ctx: 16 (over y, x), ch: 8 (over z, core).
Axes of the slice: x: 4, y: 4, z: 4, core: 2. Of those that a mesh axis runs over, the one named last changes fastest.
Arguments:
- projected: bfloat16 [3, 16384, 1024], P(None, 'ctx', 'ch'), may hold values from -6 to 6
- short_taps: float32 [3, 3, 1024], P(None, None, 'ch'), may hold values from -3 to 3
- long_filter: float32 [16384, 1024], P('ctx', 'ch'), may hold values from -1 to 1
- grad_mixed: bfloat16 [16384, 1024], P('ctx', 'ch'), may hold values from -6 to 6
Outputs:
- mixed: bfloat16 [16384, 1024], P('ctx', 'ch')
- grad_streams: bfloat16 [3, 16384, 1024], P(None, 'ctx', 'ch')
- grad_filter: float32 [16384, 1024], P('ctx', 'ch')
The draws below stay inside these ranges and needn't reach their ends.
All inputs are finite; a program needn't handle non-finite values.
Results may differ from the reference program's by a relative error of at most 0.0011.
Values may be sent and summed in bfloat16 or wider, within the bound.
A program may use at most 128 MiB of HBM per device.

```python
import jax
import jax.numpy as jnp

SLAB_CHANNELS = 1024
SEQUENCE_TOKENS = 16384


def draw_long_filter(key, part):
    random_subkeys = jax.random.split(key, 5)
    fast_share = 0.5
    chooser = jax.random.uniform(random_subkeys[0], (SLAB_CHANNELS,))
    spread_part = jax.random.uniform(random_subkeys[1], (SLAB_CHANNELS,))
    is_fast = chooser < fast_share
    decay_len = jnp.where(is_fast, 20.0 * 2.0 ** spread_part, SEQUENCE_TOKENS * 2.0 ** (2.0 * spread_part - 1.0))
    step_index = jnp.arange(SEQUENCE_TOKENS, dtype=jnp.int32)
    spike_position = jax.random.randint(random_subkeys[2], (4,), 0, SEQUENCE_TOKENS)
    spike_height = jax.random.uniform(random_subkeys[3], (4, SLAB_CHANNELS), minval=0.2, maxval=0.5)
    decay_profile = jnp.exp(-step_index.astype(jnp.float32)[:, None] / decay_len[None, :])
    for spike_pulse in range(4):
        post_spike_decay = (step_index >= spike_position[spike_pulse]).astype(jnp.float32)
        decay_profile = decay_profile * (1.0 - spike_height[spike_pulse][None, :] * post_spike_decay[:, None])
    amplitude = 1.0 / jnp.sqrt(jnp.minimum(decay_len, SEQUENCE_TOKENS * 1.0))
    rough_part = jnp.clip(jax.random.normal(random_subkeys[4], (SEQUENCE_TOKENS, SLAB_CHANNELS)), -4.0, 4.0)
    return (rough_part * decay_profile * amplitude[None, :]).astype(jnp.float32)


def level_of(key, extent, cuts, low, top_value):
    gain, own = 1.0, jax.random.fold_in(key, 6)
    for axis_at, shards_of in cuts:
        steps = jnp.exp(jax.random.uniform(jax.random.fold_in(own, axis_at), (shards_of,), jnp.float32, low / len(cuts), top_value / len(cuts)))
        gain = gain * jnp.repeat(steps, extent[axis_at] // shards_of).reshape([-1 if axis == axis_at else 1 for axis in range(len(extent))])
    return gain


def bell_draw(key, shape, width, most, cuts=(), kind=jnp.bfloat16):
    result = jax.random.normal(key, shape, jnp.float32) * width
    if len(cuts) > 0:
        result = level_of(key, shape, cuts, -0.22, 0.18) * result
    return jnp.clip(result, min=-most, max=most).astype(kind)


def setup_inputs(seed: int = 0) -> dict:
    keys = jax.random.split(jax.random.key(seed), 5)
    projected = bell_draw(keys[0], (3, SEQUENCE_TOKENS, SLAB_CHANNELS), 1.0, 6.0, ((1, 16), (2, 8)))
    short_taps = bell_draw(keys[1], (3, 3, SLAB_CHANNELS), 0.6, 3.0, ((2, 8),), jnp.float32)
    long_filter = draw_long_filter(jax.random.fold_in(keys[4], 71), 0)
    grad_mixed = bell_draw(keys[3], (SEQUENCE_TOKENS, SLAB_CHANNELS), 1.0, 6.0, ((0, 16), (1, 8)))
    return dict(projected=projected, short_taps=short_taps, long_filter=long_filter, grad_mixed=grad_mixed)


def causal_taps(projected, short_taps):
    streams = projected.astype(jnp.float32)
    length_tok = streams.shape[1]
    padded = jnp.pad(streams, ((0, 0), (2, 0), (0, 0)))
    return short_taps[:, 0][:, None, :] * streams + short_taps[:, 1][:, None, :] * padded[:, 1:length_tok + 1] + short_taps[:, 2][:, None, :] * padded[:, 0:length_tok]

def long_products(filter_block, key_value, back_gated):
    span_len = 2 * SEQUENCE_TOKENS
    filter_spec = jnp.fft.rfft(filter_block, n=span_len, axis=0)
    value_spec = jnp.fft.rfft(key_value, n=span_len, axis=0)
    back_spec = jnp.fft.rfft(back_gated, n=span_len, axis=0)
    conv_out = jnp.fft.irfft(filter_spec * value_spec, n=span_len, axis=0)[:SEQUENCE_TOKENS]
    corr_stream = jnp.fft.irfft(jnp.conj(filter_spec) * back_spec, n=span_len, axis=0)[:SEQUENCE_TOKENS]
    corr_filt = jnp.fft.irfft(jnp.conj(value_spec) * back_spec, n=span_len, axis=0)[:SEQUENCE_TOKENS]
    return (conv_out, corr_stream, corr_filt)

def reference(projected, short_taps, long_filter, grad_mixed):
    streams = causal_taps(projected, short_taps)
    query_stream, key_stream, value_stream = (streams[0], streams[1], streams[2])
    key_value = key_stream * value_stream
    grad_float = grad_mixed.astype(jnp.float32)
    back_gated = grad_float * query_stream
    width_step = min(128, SLAB_CHANNELS)
    conv_parts, stream_parts, filt_parts = ([], [], [])
    for start_col in range(0, SLAB_CHANNELS, width_step):
        stop_col = start_col + width_step
        conv_out, corr_stream, corr_filt = long_products(long_filter[:, start_col:stop_col], key_value[:, start_col:stop_col], back_gated[:, start_col:stop_col])
        conv_parts.append(conv_out)
        stream_parts.append(corr_stream)
        filt_parts.append(corr_filt)
    conv_out = jnp.concatenate(conv_parts, axis=1)
    corr_stream = jnp.concatenate(stream_parts, axis=1)
    corr_filt = jnp.concatenate(filt_parts, axis=1)
    mixed = (query_stream * conv_out).astype(jnp.bfloat16)
    grad_streams = jnp.stack([grad_float * conv_out, corr_stream * value_stream, corr_stream * key_stream]).astype(jnp.bfloat16)
    grad_filter = (corr_filt / jnp.sqrt(jnp.float32(SEQUENCE_TOKENS))).astype(jnp.float32)
    return (mixed, grad_streams, grad_filter)
```

```python
import math

import jax
import jax.numpy as jnp
import ml_dtypes
import numpy as np
from jax import lax
from jax.experimental import pallas as pl
from jax.experimental.pallas import tpu as pltpu
from jax.sharding import PartitionSpec as P

MESH = pl.DeviceIdType.MESH
SIDE = 128
DEVICES = 16
SUB = 8
BLOCKS = 8
F32, BF16 = jnp.float32, jnp.bfloat16


def halves(table):
    high = table.astype(ml_dtypes.bfloat16)
    low = (table - high.astype(np.float64)).astype(ml_dtypes.bfloat16)
    return high, low


def tables():
    index = np.arange(SIDE)
    outer = 2.0 * math.pi * ((4 * index[:, None] + 1) * index[None, :] % (4 * SIDE)) / (4 * SIDE)
    inner = 2.0 * math.pi * (index[:, None] * index[None, :] % SIDE) / SIDE
    turn = 2.0 * math.pi * ((4 * index[:, None] + 1) * index[None, :]) / (4 * SIDE * SIDE)
    first = np.concatenate([np.cos(outer), -np.sin(outer)], axis=0)
    cos, sin = np.cos(inner), np.sin(inner)
    second = np.block([[cos, -sin], [sin, cos]])
    back = np.block([[cos, sin], [-sin, cos]])
    last = np.concatenate([np.cos(outer).T, -np.sin(outer).T], axis=1) / (SIDE * SIDE)
    twist = np.stack([np.cos(turn), np.sin(turn)]).astype(np.float32)
    return halves(first) + halves(second) + halves(back) + halves(last) + (twist,)


def split(value):
    high = value.astype(BF16)
    return high, (value - high.astype(F32)).astype(BF16)


def dot(left, right):
    return jnp.dot(left, right, preferred_element_type=F32)


def left_product(high_ref, low_ref, value):
    high, low = split(value)
    return dot(high_ref[...], high) + dot(high_ref[...], low) + dot(low_ref[...], high)


def right_product(value, high_ref, low_ref):
    high, low = split(value)
    return dot(high, high_ref[...]) + dot(low, high_ref[...]) + dot(high, low_ref[...])


def kernel(
    proj, taps, filt, grad, first_h, first_l, second_h, second_l, back_h, back_l, last_h, last_l, twist,
    mixed, grad_streams, grad_filter,
    sent, got, made, home, streams, halo, spectra, send_sem, recv_sem, halo_sem,
):
    me = lax.axis_index("ctx")
    row, column = me // 4, me % 4

    def peer_of(step):
        return (row + step // 4) % 4 * 4 + (column + step % 4) % 4

    def copy_to(message, source, target, peer):
        return pltpu.make_async_remote_copy(
            src_ref=source.at[peer], dst_ref=target.at[me],
            send_sem=send_sem.at[message, peer], recv_sem=recv_sem.at[message, me],
            device_id={"ctx": peer}, device_id_type=MESH,
        )

    def copy_from(message, source, target, peer):
        return pltpu.make_async_remote_copy(
            src_ref=source.at[peer], dst_ref=target.at[peer],
            send_sem=send_sem.at[message, peer], recv_sem=recv_sem.at[message, peer],
            device_id={"ctx": peer}, device_id_type=MESH,
        )

    def each_peer(action):
        def body(step, carry):
            action(peer_of(step))
            return carry
        lax.fori_loop(1, DEVICES, body, 0)

    pairs = [(sent.at[m], got.at[m]) for m in range(3)] + [(made.at[m], home.at[m]) for m in range(3)]

    def send(message):
        source, target = pairs[message]
        each_peer(lambda peer: copy_to(message, source, target, peer).start())
        target[me] = source[me]

    def receive(message):
        source, target = pairs[message]
        each_peer(lambda peer: copy_from(message, source, target, peer).wait_recv())

    def rows_of(block):
        return pl.ds(pl.multiple_of(block * SIDE, SIDE), SIDE)

    def turned_out(message, block, value):
        sent[message, :, pl.ds(pl.multiple_of(block * SUB, SUB), SUB), :] = value.T.reshape(DEVICES, SUB, SIDE)

    def turned_home(message, block):
        return home[message, :, pl.ds(pl.multiple_of(block * SUB, SUB), SUB), :].reshape(SIDE, SIDE).T

    barrier = pltpu.get_barrier_semaphore()
    each_peer(lambda peer: pl.semaphore_signal(barrier, inc=1, device_id={"ctx": peer}, device_id_type=MESH))

    def filter_block(block, carry):
        turned_out(0, block, filt[rows_of(block), :])
        return carry
    lax.fori_loop(0, BLOCKS, filter_block, 0)

    pl.semaphore_wait(barrier, DEVICES - 1)
    after, before = (me + 1) % DEVICES, (me + DEVICES - 1) % DEVICES
    tail = pl.ds(BLOCKS * SIDE - 16, 16)

    def halo_copy(peer):
        return pltpu.make_async_remote_copy(
            src_ref=proj.at[:, tail, :], dst_ref=halo, send_sem=halo_sem.at[0], recv_sem=halo_sem.at[1],
            device_id={"ctx": peer}, device_id_type=MESH,
        )

    halo_copy(after).start()
    send(0)

    def short(stream, block, previous):
        now = proj[stream, rows_of(block), :].astype(F32)
        window = jnp.concatenate([previous[8:], now], axis=0)
        value = (
            taps[stream, 0:1, :] * now
            + taps[stream, 1:2, :] * window[7 : 7 + SIDE]
            + taps[stream, 2:3, :] * window[6 : 6 + SIDE]
        )
        streams[stream, rows_of(block), :] = value
        return value

    def inside(stream, block):
        return proj[stream, pl.ds(pl.multiple_of(block * SIDE - 16, 16), 16), :].astype(F32)

    def edge(stream):
        return jnp.where(me > 0, halo[stream].astype(F32), 0.0)

    def key_value(block, previous):
        turned_out(1, block, short(1, block, previous(1)) * short(2, block, previous(2)))

    def back_gated(block, previous):
        turned_out(2, block, short(0, block, previous(0)) * grad[rows_of(block), :].astype(F32))

    def later_blocks(make):
        def body(block, carry):
            make(block, lambda stream: inside(stream, block))
            return carry
        lax.fori_loop(1, BLOCKS, body, 0)

    later_blocks(key_value)
    halo_copy(before).wait_recv()
    key_value(0, edge)
    send(1)
    later_blocks(back_gated)
    back_gated(0, edge)
    send(2)

    def forward(message, pair):
        parts = [
            got[message, :, pl.ds(2 * pair + i, SUB, stride=SUB), :].reshape(SIDE, SIDE) for i in range(2)
        ]
        mixed_rows = left_product(first_h, first_l, jnp.concatenate(parts, axis=1))
        cos, sin = twist[0], twist[1]
        rows = []
        for i in range(2):
            real = mixed_rows[:SIDE, i * SIDE : (i + 1) * SIDE]
            imag = mixed_rows[SIDE:, i * SIDE : (i + 1) * SIDE]
            rows.append(jnp.concatenate([real * cos + imag * sin, imag * cos - real * sin], axis=1))
        return right_product(jnp.concatenate(rows, axis=0), second_h, second_l)

    def inverse(message, pair, real, imag):
        value = right_product(jnp.concatenate([real, imag], axis=1), back_h, back_l)
        cos, sin = twist[0], twist[1]
        columns = []
        for i in range(2):
            real = value[i * SIDE : (i + 1) * SIDE, :SIDE]
            imag = value[i * SIDE : (i + 1) * SIDE, SIDE:]
            columns.append(jnp.concatenate([real * cos - imag * sin, real * sin + imag * cos], axis=0))
        result = left_product(last_h, last_l, jnp.concatenate(columns, axis=1))
        for i in range(2):
            made[message, :, pl.ds(2 * pair + i, SUB, stride=SUB), :] = result[:, i * SIDE : (i + 1) * SIDE].reshape(
                DEVICES, SUB, SIDE
            )

    def parts_of(value):
        return value[:, :SIDE], value[:, SIDE:]

    def each_pair(action):
        def body(pair, carry):
            action(pair)
            return carry
        lax.fori_loop(0, SUB // 2, body, 0)

    def filter_pair(pair):
        spectra[0, pair] = forward(0, pair)

    def conv_pair(pair):
        value = forward(1, pair)
        spectra[1, pair] = value
        (fr, fi), (vr, vi) = parts_of(spectra[0, pair]), parts_of(value)
        inverse(0, pair, fr * vr - fi * vi, fr * vi + fi * vr)

    def stream_pair(pair):
        value = forward(2, pair)
        spectra[2, pair] = value
        (fr, fi), (br, bi) = parts_of(spectra[0, pair]), parts_of(value)
        inverse(1, pair, fr * br + fi * bi, fr * bi - fi * br)

    def filt_pair(pair):
        (vr, vi), (br, bi) = parts_of(spectra[1, pair]), parts_of(spectra[2, pair])
        inverse(2, pair, vr * br + vi * bi, vr * bi - vi * br)

    receive(0)
    each_pair(filter_pair)
    receive(1)
    each_pair(conv_pair)
    send(3)
    receive(2)
    each_pair(stream_pair)
    send(4)
    each_pair(filt_pair)
    send(5)

    def each_block(action):
        def body(block, carry):
            action(block)
            return carry
        lax.fori_loop(0, BLOCKS, body, 0)

    def conv_home(block):
        value, rows = turned_home(0, block), rows_of(block)
        mixed[rows, :] = (streams[0, rows, :] * value).astype(BF16)
        grad_streams[0, rows, :] = (grad[rows, :].astype(F32) * value).astype(BF16)

    def stream_home(block):
        value, rows = turned_home(1, block), rows_of(block)
        grad_streams[1, rows, :] = (value * streams[2, rows, :]).astype(BF16)
        grad_streams[2, rows, :] = (value * streams[1, rows, :]).astype(BF16)

    def filt_home(block):
        grad_filter[rows_of(block), :] = turned_home(2, block) * (1.0 / SIDE)

    for message, action in ((3, conv_home), (4, stream_home), (5, filt_home)):
        receive(message)
        each_block(action)
    for message in range(6):
        source, target = pairs[message]
        each_peer(lambda peer: copy_to(message, source, target, peer).wait_send())
    halo_copy(after).wait_send()


def local(projected, short_taps, long_filter, grad_mixed):
    constants = tables()
    tokens, channels = grad_mixed.shape
    in_vmem = pl.BlockSpec(memory_space=pltpu.VMEM)
    buffer = pltpu.VMEM((3, DEVICES, SUB * BLOCKS, SIDE), F32)
    return pl.pallas_call(
        kernel,
        out_shape=(
            jax.ShapeDtypeStruct((tokens, channels), BF16),
            jax.ShapeDtypeStruct((3, tokens, channels), BF16),
            jax.ShapeDtypeStruct((tokens, channels), F32),
        ),
        in_specs=[in_vmem] * (4 + len(constants)),
        out_specs=(in_vmem,) * 3,
        scratch_shapes=[
            buffer, buffer, buffer, buffer,
            pltpu.VMEM((3, tokens, channels), F32),
            pltpu.VMEM((3, 16, channels), BF16),
            pltpu.VMEM((3, SUB // 2, 2 * SIDE, 2 * SIDE), F32),
            pltpu.SemaphoreType.DMA((6, DEVICES)),
            pltpu.SemaphoreType.DMA((6, DEVICES)),
            pltpu.SemaphoreType.DMA((2,)),
        ],
        compiler_params=pltpu.CompilerParams(
            collective_id=0, has_side_effects=True, vmem_limit_bytes=48 * 1024 * 1024
        ),
    )(projected, short_taps, long_filter, grad_mixed, *[jnp.asarray(table) for table in constants])


def solution(mesh):
    in_specs = (P(None, "ctx", "ch"), P(None, None, "ch"), P("ctx", "ch"), P("ctx", "ch"))
    out_specs = (P("ctx", "ch"), P(None, "ctx", "ch"), P("ctx", "ch"))
    return jax.shard_map(local, mesh=mesh, in_specs=in_specs, out_specs=out_specs, check_vma=False)
```

```python
import math

import jax
import jax.numpy as jnp
import ml_dtypes
import numpy as np
from jax import lax
from jax.experimental import pallas as pl
from jax.experimental.pallas import tpu as pltpu
from jax.sharding import PartitionSpec as P

MESH = pl.DeviceIdType.MESH
SIDE = 128
DEVICES = 16
SUB = 8
BLOCKS = 8
F32, BF16 = jnp.float32, jnp.bfloat16


def halves(table):
    high = table.astype(ml_dtypes.bfloat16)
    low = (table - high.astype(np.float64)).astype(ml_dtypes.bfloat16)
    return high, low


def tables():
    index = np.arange(SIDE)
    outer = 2.0 * math.pi * ((4 * index[:, None] + 1) * index[None, :] % (4 * SIDE)) / (4 * SIDE)
    inner = 2.0 * math.pi * (index[:, None] * index[None, :] % SIDE) / SIDE
    turn = 2.0 * math.pi * ((4 * index[:, None] + 1) * index[None, :]) / (4 * SIDE * SIDE)
    first = np.concatenate([np.cos(outer), -np.sin(outer)], axis=0)
    cos, sin = np.cos(inner), np.sin(inner)
    second = np.block([[cos, -sin], [sin, cos]])
    back = np.block([[cos, sin], [-sin, cos]])
    last = np.concatenate([np.cos(outer).T, -np.sin(outer).T], axis=1) / (SIDE * SIDE)
    twist = np.stack([np.cos(turn), np.sin(turn)]).astype(np.float32)
    return np.stack(halves(first)), np.stack(halves(second)), np.stack(halves(back)), np.stack(halves(last)), twist


def split(value):
    high = value.astype(BF16)
    return high, (value - high.astype(F32)).astype(BF16)


def dot(left, right):
    return jnp.dot(left, right, preferred_element_type=F32)


def left_product(table, value):
    high, low = split(value)
    return dot(table[0], high) + dot(table[0], low) + dot(table[1], high)


def right_product(value, table):
    high, low = split(value)
    return dot(high, table[0]) + dot(low, table[0]) + dot(high, table[1])


def kernel(
    filt_hbm, proj_hbm, taps_hbm, grad_hbm, first_hbm, second_hbm, twist_hbm, back_hbm, last_hbm,
    mixed, grad_streams, grad_filter,
    filt, proj, taps, grad, first, second, twist, back, last,
    sent, got, made, home, streams, halo, spectra, load_sem, send_sem, recv_sem, halo_sem,
):
    loads = [
        pltpu.make_async_copy(source, target, load_sem.at[i])
        for i, (source, target) in enumerate((
            (filt_hbm, filt), (proj_hbm, proj), (taps_hbm, taps), (grad_hbm, grad), (first_hbm, first),
            (second_hbm, second), (twist_hbm, twist), (back_hbm, back), (last_hbm, last),
        ))
    ]
    for load in loads:
        load.start()
    me = lax.axis_index("ctx")
    row, column = me // 4, me % 4

    def peer_of(step):
        return (row + step // 4) % 4 * 4 + (column + step % 4) % 4

    def copy_to(message, source, target, peer):
        return pltpu.make_async_remote_copy(
            src_ref=source.at[peer], dst_ref=target.at[me],
            send_sem=send_sem.at[message, peer], recv_sem=recv_sem.at[message, me],
            device_id={"ctx": peer}, device_id_type=MESH,
        )

    def copy_from(message, source, target, peer):
        return pltpu.make_async_remote_copy(
            src_ref=source.at[peer], dst_ref=target.at[peer],
            send_sem=send_sem.at[message, peer], recv_sem=recv_sem.at[message, peer],
            device_id={"ctx": peer}, device_id_type=MESH,
        )

    def each_peer(action):
        def body(step, carry):
            action(peer_of(step))
            return carry
        lax.fori_loop(1, DEVICES, body, 0)

    pairs = [(sent.at[m], got.at[m]) for m in range(3)] + [(made.at[m], home.at[m]) for m in range(3)]

    def send(message):
        source, target = pairs[message]
        each_peer(lambda peer: copy_to(message, source, target, peer).start())
        target[me] = source[me]

    def receive(message):
        source, target = pairs[message]
        each_peer(lambda peer: copy_from(message, source, target, peer).wait_recv())

    def rows_of(block):
        return pl.ds(pl.multiple_of(block * SIDE, SIDE), SIDE)

    def turned_out(message, block, value):
        sent[message, :, pl.ds(pl.multiple_of(block * SUB, SUB), SUB), :] = value.T.reshape(DEVICES, SUB, SIDE)

    def turned_home(message, block):
        return home[message, :, pl.ds(pl.multiple_of(block * SUB, SUB), SUB), :].reshape(SIDE, SIDE).T

    barrier = pltpu.get_barrier_semaphore()
    each_peer(lambda peer: pl.semaphore_signal(barrier, inc=1, device_id={"ctx": peer}, device_id_type=MESH))

    loads[0].wait()

    def filter_block(block, carry):
        turned_out(0, block, filt[rows_of(block), :])
        return carry
    lax.fori_loop(0, BLOCKS, filter_block, 0)

    pl.semaphore_wait(barrier, DEVICES - 1)
    loads[1].wait()
    after, before = (me + 1) % DEVICES, (me + DEVICES - 1) % DEVICES
    tail = pl.ds(BLOCKS * SIDE - 16, 16)

    def halo_copy(peer):
        return pltpu.make_async_remote_copy(
            src_ref=proj.at[:, tail, :], dst_ref=halo, send_sem=halo_sem.at[0], recv_sem=halo_sem.at[1],
            device_id={"ctx": peer}, device_id_type=MESH,
        )

    halo_copy(after).start()
    send(0)

    def short(stream, block, previous):
        now = proj[stream, rows_of(block), :].astype(F32)
        window = jnp.concatenate([previous[8:], now], axis=0)
        value = (
            taps[stream, 0:1, :] * now
            + taps[stream, 1:2, :] * window[7 : 7 + SIDE]
            + taps[stream, 2:3, :] * window[6 : 6 + SIDE]
        )
        streams[stream, rows_of(block), :] = value
        return value

    def inside(stream, block):
        return proj[stream, pl.ds(pl.multiple_of(block * SIDE - 16, 16), 16), :].astype(F32)

    def edge(stream):
        return jnp.where(me > 0, halo[stream].astype(F32), 0.0)

    def key_value(block, previous):
        turned_out(1, block, short(1, block, previous(1)) * short(2, block, previous(2)))

    def back_gated(block, previous):
        turned_out(2, block, short(0, block, previous(0)) * grad[rows_of(block), :].astype(F32))

    def later_blocks(make):
        def body(block, carry):
            make(block, lambda stream: inside(stream, block))
            return carry
        lax.fori_loop(1, BLOCKS, body, 0)

    loads[2].wait()
    later_blocks(key_value)
    halo_copy(before).wait_recv()
    key_value(0, edge)
    send(1)
    loads[3].wait()
    later_blocks(back_gated)
    back_gated(0, edge)
    send(2)

    def forward(message, pair):
        parts = [
            got[message, :, pl.ds(2 * pair + i, SUB, stride=SUB), :].reshape(SIDE, SIDE) for i in range(2)
        ]
        mixed_rows = left_product(first, jnp.concatenate(parts, axis=1))
        cos, sin = twist[0], twist[1]
        rows = []
        for i in range(2):
            real = mixed_rows[:SIDE, i * SIDE : (i + 1) * SIDE]
            imag = mixed_rows[SIDE:, i * SIDE : (i + 1) * SIDE]
            rows.append(jnp.concatenate([real * cos + imag * sin, imag * cos - real * sin], axis=1))
        return right_product(jnp.concatenate(rows, axis=0), second)

    def inverse(message, pair, real, imag):
        value = right_product(jnp.concatenate([real, imag], axis=1), back)
        cos, sin = twist[0], twist[1]
        columns = []
        for i in range(2):
            real = value[i * SIDE : (i + 1) * SIDE, :SIDE]
            imag = value[i * SIDE : (i + 1) * SIDE, SIDE:]
            columns.append(jnp.concatenate([real * cos - imag * sin, real * sin + imag * cos], axis=0))
        result = left_product(last, jnp.concatenate(columns, axis=1))
        for i in range(2):
            made[message, :, pl.ds(2 * pair + i, SUB, stride=SUB), :] = result[:, i * SIDE : (i + 1) * SIDE].reshape(
                DEVICES, SUB, SIDE
            )

    def parts_of(value):
        return value[:, :SIDE], value[:, SIDE:]

    def each_pair(action):
        def body(pair, carry):
            action(pair)
            return carry
        lax.fori_loop(0, SUB // 2, body, 0)

    def filter_pair(pair):
        spectra[0, pair] = forward(0, pair)

    def conv_pair(pair):
        value = forward(1, pair)
        spectra[1, pair] = value
        (fr, fi), (vr, vi) = parts_of(spectra[0, pair]), parts_of(value)
        inverse(0, pair, fr * vr - fi * vi, fr * vi + fi * vr)

    def stream_pair(pair):
        value = forward(2, pair)
        spectra[2, pair] = value
        (fr, fi), (br, bi) = parts_of(spectra[0, pair]), parts_of(value)
        inverse(1, pair, fr * br + fi * bi, fr * bi - fi * br)

    def filt_pair(pair):
        (vr, vi), (br, bi) = parts_of(spectra[1, pair]), parts_of(spectra[2, pair])
        inverse(2, pair, vr * br + vi * bi, vr * bi - vi * br)

    for load in loads[4:]:
        load.wait()
    receive(0)
    each_pair(filter_pair)
    receive(1)
    each_pair(conv_pair)
    send(3)
    receive(2)
    each_pair(stream_pair)
    send(4)
    each_pair(filt_pair)
    send(5)

    def each_block(action):
        def body(block, carry):
            action(block)
            return carry
        lax.fori_loop(0, BLOCKS, body, 0)

    def conv_home(block):
        value, rows = turned_home(0, block), rows_of(block)
        mixed[rows, :] = (streams[0, rows, :] * value).astype(BF16)
        grad_streams[0, rows, :] = (grad[rows, :].astype(F32) * value).astype(BF16)

    def stream_home(block):
        value, rows = turned_home(1, block), rows_of(block)
        grad_streams[1, rows, :] = (value * streams[2, rows, :]).astype(BF16)
        grad_streams[2, rows, :] = (value * streams[1, rows, :]).astype(BF16)

    def filt_home(block):
        grad_filter[rows_of(block), :] = turned_home(2, block) * (1.0 / SIDE)

    for message, action in ((3, conv_home), (4, stream_home), (5, filt_home)):
        receive(message)
        each_block(action)
    for message in range(6):
        source, target = pairs[message]
        each_peer(lambda peer: copy_to(message, source, target, peer).wait_send())
    halo_copy(after).wait_send()


def write_out(mixed, grad_streams, grad_filter, mixed_hbm, grad_streams_hbm, grad_filter_hbm, sems):
    copies = [
        pltpu.make_async_copy(source, target, sems.at[i])
        for i, (source, target) in enumerate((
            (grad_streams, grad_streams_hbm), (grad_filter, grad_filter_hbm), (mixed, mixed_hbm),
        ))
    ]
    for copy in copies:
        copy.start()
    for copy in copies:
        copy.wait()


def local(projected, short_taps, long_filter, grad_mixed):
    first, second, back, last, twist = (jnp.asarray(table) for table in tables())
    operands = (long_filter, projected, short_taps, grad_mixed, first, second, twist, back, last)
    tokens, channels = grad_mixed.shape
    in_vmem = pl.BlockSpec(memory_space=pltpu.VMEM)
    in_hbm = pl.BlockSpec(memory_space=pltpu.MemorySpace.HBM)
    buffer = pltpu.VMEM((3, DEVICES, SUB * BLOCKS, SIDE), F32)
    out_shape = (
        jax.ShapeDtypeStruct((tokens, channels), BF16),
        jax.ShapeDtypeStruct((3, tokens, channels), BF16),
        jax.ShapeDtypeStruct((tokens, channels), F32),
    )
    results = pl.pallas_call(
        kernel,
        out_shape=out_shape,
        in_specs=[in_hbm] * len(operands),
        out_specs=(in_vmem,) * 3,
        scratch_shapes=[pltpu.VMEM(operand.shape, operand.dtype) for operand in operands]
        + [
            buffer, buffer, buffer, buffer,
            pltpu.VMEM((3, tokens, channels), F32),
            pltpu.VMEM((3, 16, channels), BF16),
            pltpu.VMEM((3, SUB // 2, 2 * SIDE, 2 * SIDE), F32),
            pltpu.SemaphoreType.DMA((len(operands),)),
            pltpu.SemaphoreType.DMA((6, DEVICES)),
            pltpu.SemaphoreType.DMA((6, DEVICES)),
            pltpu.SemaphoreType.DMA((2,)),
        ],
        compiler_params=pltpu.CompilerParams(
            collective_id=0, has_side_effects=True, vmem_limit_bytes=40 * 1024 * 1024
        ),
    )(*[pltpu.with_memory_space_constraint(operand, pltpu.MemorySpace.HBM) for operand in operands])
    return pl.pallas_call(
        write_out,
        out_shape=out_shape,
        in_specs=[in_vmem] * 3,
        out_specs=(in_hbm,) * 3,
        scratch_shapes=[pltpu.SemaphoreType.DMA((3,))],
    )(*[pltpu.with_memory_space_constraint(result, pltpu.VMEM) for result in results])


def solution(mesh):
    in_specs = (P(None, "ctx", "ch"), P(None, None, "ch"), P("ctx", "ch"), P("ctx", "ch"))
    out_specs = (P("ctx", "ch"), P(None, "ctx", "ch"), P("ctx", "ch"))
    return jax.shard_map(local, mesh=mesh, in_specs=in_specs, out_specs=out_specs, check_vma=False)
```

```python
import math

import jax
import jax.numpy as jnp
import ml_dtypes
import numpy as np
from jax import lax
from jax.experimental import pallas as pl
from jax.experimental.pallas import tpu as pltpu
from jax.sharding import PartitionSpec as P

MESH = pl.DeviceIdType.MESH
SIDE = 128
DEVICES = 16
SUB = 8
BLOCKS = 8
OFFSET = 1.0 / 64.0
F32, BF16 = jnp.float32, jnp.bfloat16


def halves(table):
    high = table.astype(ml_dtypes.bfloat16)
    low = (table - high.astype(np.float64)).astype(ml_dtypes.bfloat16)
    return high, low


def tables():
    index = np.arange(SIDE)
    outer = 2.0 * math.pi * ((4 * index[:, None] + 1) * index[None, :] % (4 * SIDE)) / (4 * SIDE)
    inner = 2.0 * math.pi * (index[:, None] * index[None, :] % SIDE) / SIDE
    turn = 2.0 * math.pi * ((4 * index[:, None] + 1) * index[None, :]) / (4 * SIDE * SIDE)
    first = np.concatenate([np.cos(outer), -np.sin(outer)], axis=0)
    cos, sin = np.cos(inner), np.sin(inner)
    second = np.block([[cos, -sin], [sin, cos]])
    back = np.block([[cos, sin], [-sin, cos]])
    last = np.concatenate([np.cos(outer).T, -np.sin(outer).T], axis=1) / (SIDE * SIDE)
    twist = np.stack([np.cos(turn), np.sin(turn)]).astype(np.float32)
    return np.stack(halves(first)), np.stack(halves(second)), np.stack(halves(back)), np.stack(halves(last)), twist


def split(value):
    high = value.astype(BF16)
    return high, (value - high.astype(F32)).astype(BF16)


def dot(left, right):
    return jnp.dot(left, right, preferred_element_type=F32)


def left_product(table, value):
    high, low = split(value)
    return dot(table[0], high) + dot(table[0], low) + dot(table[1], high)


def right_product(value, table):
    high, low = split(value)
    return dot(high, table[0]) + dot(low, table[0]) + dot(high, table[1])


def scale_of(largest):
    return 8.0 / jnp.maximum(largest, 1e-30)


def coded(value, scale):
    base = jnp.abs(value) * scale + 8.0 * OFFSET
    two = base * base
    four = two * two
    eight = four * four
    sixteen = eight * eight
    power = sixteen * sixteen * eight
    return jnp.where(value < 0.0, -power, power)


def decoded(code, largest):
    root = jnp.exp2(jnp.log2(jnp.abs(code)) * (1.0 / 40.0))
    size = root * (largest * 0.125) - largest * OFFSET
    return jnp.where(code < 0.0, -size, size)


def kernel(
    filt_hbm, proj_hbm, taps_hbm, grad_hbm, first_hbm, second_hbm, twist_hbm, back_hbm, last_hbm,
    mixed, grad_streams, grad_filter,
    filt, proj, taps, grad, first, second, twist, back, last,
    sent, got, made, home, scales_out, scales_in, plain, gathered, results, streams, halo, spectra,
    load_sem, send_sem, recv_sem, halo_sem,
):
    loads = [
        pltpu.make_async_copy(source, target, load_sem.at[i])
        for i, (source, target) in enumerate((
            (filt_hbm, filt), (proj_hbm, proj), (taps_hbm, taps), (grad_hbm, grad), (first_hbm, first),
            (second_hbm, second), (twist_hbm, twist), (back_hbm, back), (last_hbm, last),
        ))
    ]
    for load in loads:
        load.start()
    me = lax.axis_index("ctx")
    row, column = me // 4, me % 4

    def peer_of(step):
        return (row + step // 4) % 4 * 4 + (column + step % 4) % 4

    def each_peer(action):
        def body(step, carry):
            action(peer_of(step))
            return carry
        lax.fori_loop(1, DEVICES, body, 0)

    pairs = [(sent.at[m], got.at[m]) for m in range(3)] + [(made.at[m], home.at[m]) for m in range(3)]
    pairs += [(scales_out.at[m], scales_in.at[m]) for m in range(6)]

    def copy_to(message, peer):
        source, target = pairs[message]
        return pltpu.make_async_remote_copy(
            src_ref=source.at[peer], dst_ref=target.at[me],
            send_sem=send_sem.at[message, peer], recv_sem=recv_sem.at[message, me],
            device_id={"ctx": peer}, device_id_type=MESH,
        )

    def copy_from(message, peer):
        source, target = pairs[message]
        return pltpu.make_async_remote_copy(
            src_ref=source.at[peer], dst_ref=target.at[peer],
            send_sem=send_sem.at[message, peer], recv_sem=recv_sem.at[message, peer],
            device_id={"ctx": peer}, device_id_type=MESH,
        )

    def send(message):
        def start(peer):
            copy_to(message + 6, peer).start()
            copy_to(message, peer).start()
        each_peer(start)
        for source, target in (pairs[message], pairs[message + 6]):
            target[me] = source[me]

    def receive(message):
        def wait(peer):
            copy_from(message + 6, peer).wait_recv()
            copy_from(message, peer).wait_recv()
        each_peer(wait)

    def rows_of(block):
        return pl.ds(pl.multiple_of(block * SIDE, SIDE), SIDE)

    def code_rows(pair):
        return pl.ds(pl.multiple_of(pair * 2 * SUB, 2 * SUB), 2 * SUB)

    def turned_out(message, source):
        largest = jnp.max(jnp.abs(source[...]), axis=0, keepdims=True)
        scales_out[message] = jnp.broadcast_to(largest[None], (DEVICES, 1, SIDE))
        scale = scale_of(largest)

        def body(pair, carry):
            turned = [
                coded(source[rows_of(2 * pair + i), :], scale).T.reshape(DEVICES, SUB, SIDE) for i in range(2)
            ]
            sent[message, :, code_rows(pair), :] = jnp.concatenate(turned, axis=1).astype(BF16)
            return carry
        lax.fori_loop(0, BLOCKS // 2, body, 0)

    barrier = pltpu.get_barrier_semaphore()
    each_peer(lambda peer: pl.semaphore_signal(barrier, inc=1, device_id={"ctx": peer}, device_id_type=MESH))
    loads[0].wait()
    turned_out(0, filt)
    pl.semaphore_wait(barrier, DEVICES - 1)
    loads[1].wait()
    after, before = (me + 1) % DEVICES, (me + DEVICES - 1) % DEVICES
    tail = pl.ds(BLOCKS * SIDE - 16, 16)

    def halo_copy(peer):
        return pltpu.make_async_remote_copy(
            src_ref=proj.at[:, tail, :], dst_ref=halo, send_sem=halo_sem.at[0], recv_sem=halo_sem.at[1],
            device_id={"ctx": peer}, device_id_type=MESH,
        )

    halo_copy(after).start()
    send(0)

    def short(stream, block, previous):
        now = proj[stream, rows_of(block), :].astype(F32)
        window = jnp.concatenate([previous[8:], now], axis=0)
        value = (
            taps[stream, 0:1, :] * now
            + taps[stream, 1:2, :] * window[7 : 7 + SIDE]
            + taps[stream, 2:3, :] * window[6 : 6 + SIDE]
        )
        streams[stream, rows_of(block), :] = value
        return value

    def inside(stream, block):
        return proj[stream, pl.ds(pl.multiple_of(block * SIDE - 16, 16), 16), :].astype(F32)

    def edge(stream):
        return jnp.where(me > 0, halo[stream].astype(F32), 0.0)

    def key_value(block, previous):
        plain[rows_of(block), :] = short(1, block, previous(1)) * short(2, block, previous(2))

    def back_gated(block, previous):
        plain[rows_of(block), :] = short(0, block, previous(0)) * grad[rows_of(block), :].astype(F32)

    def later_blocks(make):
        def body(block, carry):
            make(block, lambda stream: inside(stream, block))
            return carry
        lax.fori_loop(1, BLOCKS, body, 0)

    loads[2].wait()
    later_blocks(key_value)
    halo_copy(before).wait_recv()
    key_value(0, edge)
    turned_out(1, plain)
    send(1)
    loads[3].wait()
    later_blocks(back_gated)
    back_gated(0, edge)
    turned_out(2, plain)
    send(2)

    def lane_is_own(shape, axis):
        lane = lax.broadcasted_iota(jnp.int32, shape, len(shape) - 1)
        return lane == SUB * me + lax.broadcasted_iota(jnp.int32, shape, axis)

    def gather(message):
        receive(message)
        shape = (DEVICES, SUB, SIDE)
        rows = jnp.broadcast_to(scales_in[message], shape)
        largest = jnp.sum(jnp.where(lane_is_own(shape, 1), rows, 0.0), axis=2, keepdims=True)
        for source in range(DEVICES):
            code = got[message, source].astype(F32).reshape(BLOCKS, SUB, SIDE)
            gathered[source] = decoded(code, largest[source : source + 1]).reshape(BLOCKS * SUB, SIDE)

    def scatter(message):
        for target in range(DEVICES):
            value = results[target].reshape(BLOCKS, SUB, SIDE)
            largest = jnp.max(jnp.max(jnp.abs(value), axis=0), axis=1, keepdims=True)
            spread = jnp.where(lane_is_own((SUB, SIDE), 0), largest, 0.0)
            scales_out[message, target] = jnp.sum(spread, axis=0, keepdims=True)
            made[message - 3, target] = coded(value, scale_of(largest)[None]).reshape(BLOCKS * SUB, SIDE).astype(BF16)
        send(message)

    def forward(pair):
        parts = [gathered[:, pl.ds(2 * pair + i, SUB, stride=SUB), :].reshape(SIDE, SIDE) for i in range(2)]
        mixed_rows = left_product(first, jnp.concatenate(parts, axis=1))
        cos, sin = twist[0], twist[1]
        rows = []
        for i in range(2):
            real = mixed_rows[:SIDE, i * SIDE : (i + 1) * SIDE]
            imag = mixed_rows[SIDE:, i * SIDE : (i + 1) * SIDE]
            rows.append(jnp.concatenate([real * cos + imag * sin, imag * cos - real * sin], axis=1))
        return right_product(jnp.concatenate(rows, axis=0), second)

    def inverse(pair, real, imag):
        value = right_product(jnp.concatenate([real, imag], axis=1), back)
        cos, sin = twist[0], twist[1]
        columns = []
        for i in range(2):
            real = value[i * SIDE : (i + 1) * SIDE, :SIDE]
            imag = value[i * SIDE : (i + 1) * SIDE, SIDE:]
            columns.append(jnp.concatenate([real * cos - imag * sin, real * sin + imag * cos], axis=0))
        result = left_product(last, jnp.concatenate(columns, axis=1))
        for i in range(2):
            results[:, pl.ds(2 * pair + i, SUB, stride=SUB), :] = result[:, i * SIDE : (i + 1) * SIDE].reshape(
                DEVICES, SUB, SIDE
            )

    def parts_of(value):
        return value[:, :SIDE], value[:, SIDE:]

    def each_pair(action):
        for pair in range(SUB // 2):
            action(pair)

    def filter_pair(pair):
        spectra[0, pair] = forward(pair)

    def conv_pair(pair):
        value = forward(pair)
        spectra[1, pair] = value
        (fr, fi), (vr, vi) = parts_of(spectra[0, pair]), parts_of(value)
        inverse(pair, fr * vr - fi * vi, fr * vi + fi * vr)

    def stream_pair(pair):
        value = forward(pair)
        spectra[2, pair] = value
        (fr, fi), (br, bi) = parts_of(spectra[0, pair]), parts_of(value)
        inverse(pair, fr * br + fi * bi, fr * bi - fi * br)

    def filt_pair(pair):
        (vr, vi), (br, bi) = parts_of(spectra[1, pair]), parts_of(spectra[2, pair])
        inverse(pair, vr * br + vi * bi, vr * bi - vi * br)

    for load in loads[4:]:
        load.wait()
    gather(0)
    each_pair(filter_pair)
    gather(1)
    each_pair(conv_pair)
    scatter(3)
    gather(2)
    each_pair(stream_pair)
    scatter(4)
    each_pair(filt_pair)
    scatter(5)

    def turned_home(message, action):
        receive(message)
        largest = jnp.sum(scales_in[message], axis=0)

        def body(pair, carry):
            code = home[message - 3, :, code_rows(pair), :].astype(F32)
            for i in range(2):
                turned = code[:, i * SUB : (i + 1) * SUB, :].reshape(SIDE, SIDE).T
                action(rows_of(2 * pair + i), decoded(turned, largest))
            return carry
        lax.fori_loop(0, BLOCKS // 2, body, 0)

    def conv_home(rows, value):
        mixed[rows, :] = (streams[0, rows, :] * value).astype(BF16)
        grad_streams[0, rows, :] = (grad[rows, :].astype(F32) * value).astype(BF16)

    def stream_home(rows, value):
        grad_streams[1, rows, :] = (value * streams[2, rows, :]).astype(BF16)
        grad_streams[2, rows, :] = (value * streams[1, rows, :]).astype(BF16)

    def filt_home(rows, value):
        grad_filter[rows, :] = value * (1.0 / SIDE)

    turned_home(3, conv_home)
    turned_home(4, stream_home)
    turned_home(5, filt_home)
    for message in range(12):
        each_peer(lambda peer: copy_to(message, peer).wait_send())
    halo_copy(after).wait_send()


def write_out(mixed, grad_streams, grad_filter, mixed_hbm, grad_streams_hbm, grad_filter_hbm, sems):
    copies = [
        pltpu.make_async_copy(source, target, sems.at[i])
        for i, (source, target) in enumerate((
            (grad_streams, grad_streams_hbm), (grad_filter, grad_filter_hbm), (mixed, mixed_hbm),
        ))
    ]
    for copy in copies:
        copy.start()
    for copy in copies:
        copy.wait()


def local(projected, short_taps, long_filter, grad_mixed):
    first, second, back, last, twist = (jnp.asarray(table) for table in tables())
    operands = (long_filter, projected, short_taps, grad_mixed, first, second, twist, back, last)
    tokens, channels = grad_mixed.shape
    in_vmem = pl.BlockSpec(memory_space=pltpu.VMEM)
    in_hbm = pl.BlockSpec(memory_space=pltpu.MemorySpace.HBM)
    buffer = pltpu.VMEM((3, DEVICES, SUB * BLOCKS, SIDE), BF16)
    scales = pltpu.VMEM((6, DEVICES, 1, SIDE), F32)
    whole = pltpu.VMEM((DEVICES, SUB * BLOCKS, SIDE), F32)
    out_shape = (
        jax.ShapeDtypeStruct((tokens, channels), BF16),
        jax.ShapeDtypeStruct((3, tokens, channels), BF16),
        jax.ShapeDtypeStruct((tokens, channels), F32),
    )
    results = pl.pallas_call(
        kernel,
        out_shape=out_shape,
        in_specs=[in_hbm] * len(operands),
        out_specs=(in_vmem,) * 3,
        scratch_shapes=[pltpu.VMEM(operand.shape, operand.dtype) for operand in operands]
        + [
            buffer, buffer, buffer, buffer, scales, scales,
            pltpu.VMEM((tokens, channels), F32), whole, whole,
            pltpu.VMEM((3, tokens, channels), F32),
            pltpu.VMEM((3, 16, channels), BF16),
            pltpu.VMEM((3, SUB // 2, 2 * SIDE, 2 * SIDE), F32),
            pltpu.SemaphoreType.DMA((len(operands),)),
            pltpu.SemaphoreType.DMA((12, DEVICES)),
            pltpu.SemaphoreType.DMA((12, DEVICES)),
            pltpu.SemaphoreType.DMA((2,)),
        ],
        compiler_params=pltpu.CompilerParams(
            collective_id=0, has_side_effects=True, vmem_limit_bytes=40 * 1024 * 1024
        ),
    )(*[pltpu.with_memory_space_constraint(operand, pltpu.MemorySpace.HBM) for operand in operands])
    return pl.pallas_call(
        write_out,
        out_shape=out_shape,
        in_specs=[in_vmem] * 3,
        out_specs=(in_hbm,) * 3,
        scratch_shapes=[pltpu.SemaphoreType.DMA((3,))],
    )(*[pltpu.with_memory_space_constraint(result, pltpu.VMEM) for result in results])


def solution(mesh):
    in_specs = (P(None, "ctx", "ch"), P(None, None, "ch"), P("ctx", "ch"), P("ctx", "ch"))
    out_specs = (P("ctx", "ch"), P(None, "ctx", "ch"), P("ctx", "ch"))
    return jax.shard_map(local, mesh=mesh, in_specs=in_specs, out_specs=out_specs, check_vma=False)
```

```python
import math

import jax
import jax.numpy as jnp
import ml_dtypes
import numpy as np
from jax import lax
from jax.experimental import pallas as pl
from jax.experimental.pallas import tpu as pltpu
from jax.sharding import PartitionSpec as P

MESH = pl.DeviceIdType.MESH
SIDE = 128
DEVICES = 16
SUB = 8
BLOCKS = 8
OFFSET = 1.0 / 64.0
F32, BF16 = jnp.float32, jnp.bfloat16


def halves(table):
    high = table.astype(ml_dtypes.bfloat16)
    low = (table - high.astype(np.float64)).astype(ml_dtypes.bfloat16)
    return high, low


def tables():
    index = np.arange(SIDE)
    outer = 2.0 * math.pi * ((4 * index[:, None] + 1) * index[None, :] % (4 * SIDE)) / (4 * SIDE)
    inner = 2.0 * math.pi * (index[:, None] * index[None, :] % SIDE) / SIDE
    turn = 2.0 * math.pi * ((4 * index[:, None] + 1) * index[None, :]) / (4 * SIDE * SIDE)
    first = np.concatenate([np.cos(outer), -np.sin(outer)], axis=0)
    cos, sin = np.cos(inner), np.sin(inner)
    second = np.block([[cos, -sin], [sin, cos]])
    back = np.block([[cos, sin], [-sin, cos]])
    last = np.concatenate([np.cos(outer).T, -np.sin(outer).T], axis=1) / (SIDE * SIDE)
    twist = np.stack([np.cos(turn), np.sin(turn)]).astype(np.float32)
    return np.stack(halves(first)), np.stack(halves(second)), np.stack(halves(back)), np.stack(halves(last)), twist


def split(value):
    high = value.astype(BF16)
    return high, (value - high.astype(F32)).astype(BF16)


def dot(left, right):
    return jnp.dot(left, right, preferred_element_type=F32)


def left_product(table, value):
    high, low = split(value)
    return dot(table[0], high) + dot(table[0], low) + dot(table[1], high)


def right_product(value, table):
    high, low = split(value)
    return dot(high, table[0]) + dot(low, table[0]) + dot(high, table[1])


def scale_of(largest):
    return 8.0 / jnp.maximum(largest, 1e-30)


def coded(value, scale):
    base = jnp.abs(value) * scale + 8.0 * OFFSET
    two = base * base
    four = two * two
    eight = four * four
    sixteen = eight * eight
    power = sixteen * sixteen * eight
    return jnp.where(value < 0.0, -power, power)


def decoded(code, largest):
    root = jnp.exp2(jnp.log2(jnp.abs(code)) * (1.0 / 40.0))
    size = root * (largest * 0.125) - largest * OFFSET
    return jnp.where(code < 0.0, -size, size)


def kernel(
    filt_hbm, proj_hbm, taps_hbm, grad_hbm, first_hbm, second_hbm, twist_hbm, back_hbm, last_hbm,
    mixed, grad_streams, grad_filter,
    filt, proj, taps, grad, first, second, twist, back, last,
    sent, got, made, home, scales_out, scales_in, plain, gathered, results, streams, halo, spectra,
    load_sem, send_sem, recv_sem, halo_sem,
):
    loads = [
        pltpu.make_async_copy(source, target, load_sem.at[i])
        for i, (source, target) in enumerate((
            (filt_hbm, filt), (proj_hbm, proj), (taps_hbm, taps), (grad_hbm, grad), (first_hbm, first),
            (second_hbm, second), (twist_hbm, twist), (back_hbm, back), (last_hbm, last),
        ))
    ]
    for load in loads:
        load.start()
    me = lax.axis_index("ctx")
    row, column = me // 4, me % 4

    def peer_of(step):
        return (row + step // 4) % 4 * 4 + (column + step % 4) % 4

    peers = [peer_of(step) for step in range(1, DEVICES)]

    def each_peer(action):
        for peer in peers:
            action(peer)

    pairs = [(sent.at[m], got.at[m]) for m in range(3)] + [(made.at[m], home.at[m]) for m in range(3)]
    pairs += [(scales_out.at[m], scales_in.at[m]) for m in range(6)]

    def copy_to(message, peer):
        source, target = pairs[message]
        return pltpu.make_async_remote_copy(
            src_ref=source.at[peer], dst_ref=target.at[me],
            send_sem=send_sem.at[message], recv_sem=recv_sem.at[message],
            device_id={"ctx": peer}, device_id_type=MESH,
        )

    def all_copies(message):
        source, target = pairs[message]
        every = pl.ds(0, DEVICES - 1)
        return pltpu.make_async_remote_copy(
            src_ref=source.at[every], dst_ref=target.at[every],
            send_sem=send_sem.at[message], recv_sem=recv_sem.at[message],
            device_id={"ctx": peers[0]}, device_id_type=MESH,
        )

    def send(message):
        def start(peer):
            copy_to(message + 6, peer).start()
            copy_to(message, peer).start()
        each_peer(start)
        for source, target in (pairs[message], pairs[message + 6]):
            target[me] = source[me]

    def receive(message):
        all_copies(message + 6).wait_recv()
        all_copies(message).wait_recv()

    def rows_of(block):
        return pl.ds(pl.multiple_of(block * SIDE, SIDE), SIDE)

    def code_rows(pair):
        return pl.ds(pl.multiple_of(pair * 2 * SUB, 2 * SUB), 2 * SUB)

    def turned_out(message, source):
        largest = jnp.max(jnp.abs(source[...]), axis=0, keepdims=True)
        scales_out[message] = jnp.broadcast_to(largest[None], (DEVICES, 1, SIDE))
        scale = scale_of(largest)

        def body(pair, carry):
            turned = [
                coded(source[rows_of(2 * pair + i), :], scale).T.reshape(DEVICES, SUB, SIDE) for i in range(2)
            ]
            sent[message, :, code_rows(pair), :] = jnp.concatenate(turned, axis=1).astype(BF16)
            return carry
        lax.fori_loop(0, BLOCKS // 2, body, 0)

    barrier = pltpu.get_barrier_semaphore()
    each_peer(lambda peer: pl.semaphore_signal(barrier, inc=1, device_id={"ctx": peer}, device_id_type=MESH))
    loads[0].wait()
    turned_out(0, filt)
    pl.semaphore_wait(barrier, DEVICES - 1)
    loads[1].wait()
    after, before = (me + 1) % DEVICES, (me + DEVICES - 1) % DEVICES
    tail = pl.ds(BLOCKS * SIDE - 16, 16)

    def halo_copy(peer):
        return pltpu.make_async_remote_copy(
            src_ref=proj.at[:, tail, :], dst_ref=halo, send_sem=halo_sem.at[0], recv_sem=halo_sem.at[1],
            device_id={"ctx": peer}, device_id_type=MESH,
        )

    halo_copy(after).start()
    send(0)

    def short(stream, block, previous):
        now = proj[stream, rows_of(block), :].astype(F32)
        window = jnp.concatenate([previous[8:], now], axis=0)
        value = (
            taps[stream, 0:1, :] * now
            + taps[stream, 1:2, :] * window[7 : 7 + SIDE]
            + taps[stream, 2:3, :] * window[6 : 6 + SIDE]
        )
        streams[stream, rows_of(block), :] = value
        return value

    def inside(stream, block):
        return proj[stream, pl.ds(pl.multiple_of(block * SIDE - 16, 16), 16), :].astype(F32)

    def edge(stream):
        return jnp.where(me > 0, halo[stream].astype(F32), 0.0)

    def key_value(block, previous):
        plain[rows_of(block), :] = short(1, block, previous(1)) * short(2, block, previous(2))

    def back_gated(block, previous):
        plain[rows_of(block), :] = short(0, block, previous(0)) * grad[rows_of(block), :].astype(F32)

    def later_blocks(make):
        def body(block, carry):
            make(block, lambda stream: inside(stream, block))
            return carry
        lax.fori_loop(1, BLOCKS, body, 0)

    loads[2].wait()
    later_blocks(key_value)
    halo_copy(before).wait_recv()
    key_value(0, edge)
    turned_out(1, plain)
    send(1)
    loads[3].wait()
    later_blocks(back_gated)
    back_gated(0, edge)
    turned_out(2, plain)
    send(2)

    def lane_is_own(shape, axis):
        lane = lax.broadcasted_iota(jnp.int32, shape, len(shape) - 1)
        return lane == SUB * me + lax.broadcasted_iota(jnp.int32, shape, axis)

    def gather(message):
        receive(message)
        shape = (DEVICES, SUB, SIDE)
        rows = jnp.broadcast_to(scales_in[message], shape)
        largest = jnp.sum(jnp.where(lane_is_own(shape, 1), rows, 0.0), axis=2, keepdims=True)
        for source in range(DEVICES):
            code = got[message, source].astype(F32).reshape(BLOCKS, SUB, SIDE)
            gathered[source] = decoded(code, largest[source : source + 1]).reshape(BLOCKS * SUB, SIDE)

    def scatter(message):
        for target in range(DEVICES):
            value = results[target].reshape(BLOCKS, SUB, SIDE)
            largest = jnp.max(jnp.max(jnp.abs(value), axis=0), axis=1, keepdims=True)
            spread = jnp.where(lane_is_own((SUB, SIDE), 0), largest, 0.0)
            scales_out[message, target] = jnp.sum(spread, axis=0, keepdims=True)
            made[message - 3, target] = coded(value, scale_of(largest)[None]).reshape(BLOCKS * SUB, SIDE).astype(BF16)
        send(message)

    def forward(pair):
        parts = [gathered[:, pl.ds(2 * pair + i, SUB, stride=SUB), :].reshape(SIDE, SIDE) for i in range(2)]
        mixed_rows = left_product(first, jnp.concatenate(parts, axis=1))
        cos, sin = twist[0], twist[1]
        rows = []
        for i in range(2):
            real = mixed_rows[:SIDE, i * SIDE : (i + 1) * SIDE]
            imag = mixed_rows[SIDE:, i * SIDE : (i + 1) * SIDE]
            rows.append(jnp.concatenate([real * cos + imag * sin, imag * cos - real * sin], axis=1))
        return right_product(jnp.concatenate(rows, axis=0), second)

    def inverse(pair, real, imag):
        value = right_product(jnp.concatenate([real, imag], axis=1), back)
        cos, sin = twist[0], twist[1]
        columns = []
        for i in range(2):
            real = value[i * SIDE : (i + 1) * SIDE, :SIDE]
            imag = value[i * SIDE : (i + 1) * SIDE, SIDE:]
            columns.append(jnp.concatenate([real * cos - imag * sin, real * sin + imag * cos], axis=0))
        result = left_product(last, jnp.concatenate(columns, axis=1))
        for i in range(2):
            results[:, pl.ds(2 * pair + i, SUB, stride=SUB), :] = result[:, i * SIDE : (i + 1) * SIDE].reshape(
                DEVICES, SUB, SIDE
            )

    def parts_of(value):
        return value[:, :SIDE], value[:, SIDE:]

    def each_pair(action):
        for pair in range(SUB // 2):
            action(pair)

    def filter_pair(pair):
        spectra[0, pair] = forward(pair)

    def conv_pair(pair):
        value = forward(pair)
        spectra[1, pair] = value
        (fr, fi), (vr, vi) = parts_of(spectra[0, pair]), parts_of(value)
        inverse(pair, fr * vr - fi * vi, fr * vi + fi * vr)

    def stream_pair(pair):
        value = forward(pair)
        spectra[2, pair] = value
        (fr, fi), (br, bi) = parts_of(spectra[0, pair]), parts_of(value)
        inverse(pair, fr * br + fi * bi, fr * bi - fi * br)

    def filt_pair(pair):
        (vr, vi), (br, bi) = parts_of(spectra[1, pair]), parts_of(spectra[2, pair])
        inverse(pair, vr * br + vi * bi, vr * bi - vi * br)

    for load in loads[4:]:
        load.wait()
    gather(0)
    each_pair(filter_pair)
    gather(1)
    each_pair(conv_pair)
    scatter(3)
    gather(2)
    each_pair(stream_pair)
    scatter(4)
    each_pair(filt_pair)
    scatter(5)

    def turned_home(message, action):
        receive(message)
        largest = jnp.sum(scales_in[message], axis=0)

        def body(pair, carry):
            code = home[message - 3, :, code_rows(pair), :].astype(F32)
            for i in range(2):
                turned = code[:, i * SUB : (i + 1) * SUB, :].reshape(SIDE, SIDE).T
                action(rows_of(2 * pair + i), decoded(turned, largest))
            return carry
        lax.fori_loop(0, BLOCKS // 2, body, 0)

    def conv_home(rows, value):
        mixed[rows, :] = (streams[0, rows, :] * value).astype(BF16)
        grad_streams[0, rows, :] = (grad[rows, :].astype(F32) * value).astype(BF16)

    def stream_home(rows, value):
        grad_streams[1, rows, :] = (value * streams[2, rows, :]).astype(BF16)
        grad_streams[2, rows, :] = (value * streams[1, rows, :]).astype(BF16)

    def filt_home(rows, value):
        grad_filter[rows, :] = value * (1.0 / SIDE)

    turned_home(3, conv_home)
    turned_home(4, stream_home)
    turned_home(5, filt_home)
    for message in range(12):
        all_copies(message).wait_send()
    halo_copy(after).wait_send()


def write_out(mixed, grad_streams, grad_filter, mixed_hbm, grad_streams_hbm, grad_filter_hbm, sems):
    copies = [
        pltpu.make_async_copy(source, target, sems.at[i])
        for i, (source, target) in enumerate((
            (grad_streams, grad_streams_hbm), (grad_filter, grad_filter_hbm), (mixed, mixed_hbm),
        ))
    ]
    for copy in copies:
        copy.start()
    for copy in copies:
        copy.wait()


def local(projected, short_taps, long_filter, grad_mixed):
    first, second, back, last, twist = (jnp.asarray(table) for table in tables())
    operands = (long_filter, projected, short_taps, grad_mixed, first, second, twist, back, last)
    tokens, channels = grad_mixed.shape
    in_vmem = pl.BlockSpec(memory_space=pltpu.VMEM)
    in_hbm = pl.BlockSpec(memory_space=pltpu.MemorySpace.HBM)
    buffer = pltpu.VMEM((3, DEVICES, SUB * BLOCKS, SIDE), BF16)
    scales = pltpu.VMEM((6, DEVICES, 1, SIDE), F32)
    whole = pltpu.VMEM((DEVICES, SUB * BLOCKS, SIDE), F32)
    out_shape = (
        jax.ShapeDtypeStruct((tokens, channels), BF16),
        jax.ShapeDtypeStruct((3, tokens, channels), BF16),
        jax.ShapeDtypeStruct((tokens, channels), F32),
    )
    results = pl.pallas_call(
        kernel,
        out_shape=out_shape,
        in_specs=[in_hbm] * len(operands),
        out_specs=(in_vmem,) * 3,
        scratch_shapes=[pltpu.VMEM(operand.shape, operand.dtype) for operand in operands]
        + [
            buffer, buffer, buffer, buffer, scales, scales,
            pltpu.VMEM((tokens, channels), F32), whole, whole,
            pltpu.VMEM((3, tokens, channels), F32),
            pltpu.VMEM((3, 16, channels), BF16),
            pltpu.VMEM((3, SUB // 2, 2 * SIDE, 2 * SIDE), F32),
            pltpu.SemaphoreType.DMA((len(operands),)),
            pltpu.SemaphoreType.DMA((12,)),
            pltpu.SemaphoreType.DMA((12,)),
            pltpu.SemaphoreType.DMA((2,)),
        ],
        compiler_params=pltpu.CompilerParams(
            collective_id=0, has_side_effects=True, vmem_limit_bytes=40 * 1024 * 1024
        ),
    )(*[pltpu.with_memory_space_constraint(operand, pltpu.MemorySpace.HBM) for operand in operands])
    return pl.pallas_call(
        write_out,
        out_shape=out_shape,
        in_specs=[in_vmem] * 3,
        out_specs=(in_hbm,) * 3,
        scratch_shapes=[pltpu.SemaphoreType.DMA((3,))],
    )(*[pltpu.with_memory_space_constraint(result, pltpu.VMEM) for result in results])


def solution(mesh):
    in_specs = (P(None, "ctx", "ch"), P(None, None, "ch"), P("ctx", "ch"), P("ctx", "ch"))
    out_specs = (P("ctx", "ch"), P(None, "ctx", "ch"), P("ctx", "ch"))
    return jax.shard_map(local, mesh=mesh, in_specs=in_specs, out_specs=out_specs, check_vma=False)
```

```python
import math

import jax
import jax.numpy as jnp
import ml_dtypes
import numpy as np
from jax import lax
from jax.experimental import pallas as pl
from jax.experimental.pallas import tpu as pltpu
from jax.sharding import PartitionSpec as P

MESH = pl.DeviceIdType.MESH
SIDE = 128
DEVICES = 16
SUB = 8
BLOCKS = 8
OFFSET = 1.0 / 64.0
F32, BF16 = jnp.float32, jnp.bfloat16


def halves(table):
    high = table.astype(ml_dtypes.bfloat16)
    low = (table - high.astype(np.float64)).astype(ml_dtypes.bfloat16)
    return high, low


def tables():
    index = np.arange(SIDE)
    outer = 2.0 * math.pi * ((4 * index[:, None] + 1) * index[None, :] % (4 * SIDE)) / (4 * SIDE)
    inner = 2.0 * math.pi * (index[:, None] * index[None, :] % SIDE) / SIDE
    turn = 2.0 * math.pi * ((4 * index[:, None] + 1) * index[None, :]) / (4 * SIDE * SIDE)
    first = np.concatenate([np.cos(outer), -np.sin(outer)], axis=0)
    cos, sin = np.cos(inner), np.sin(inner)
    second = np.block([[cos, -sin], [sin, cos]])
    back = np.block([[cos, sin], [-sin, cos]])
    last = np.concatenate([np.cos(outer).T, -np.sin(outer).T], axis=1) / (SIDE * SIDE)
    twist = np.stack([np.cos(turn), np.sin(turn)]).astype(np.float32)
    return np.stack(halves(first)), np.stack(halves(second)), np.stack(halves(back)), np.stack(halves(last)), twist


def split(value):
    high = value.astype(BF16)
    return high, (value - high.astype(F32)).astype(BF16)


def dot(left, right):
    return jnp.dot(left, right, preferred_element_type=F32)


def left_product(table, value):
    high, low = split(value)
    return dot(table[0], high) + dot(table[0], low) + dot(table[1], high)


def right_product(value, table):
    high, low = split(value)
    return dot(high, table[0]) + dot(low, table[0]) + dot(high, table[1])


def scale_of(largest):
    return 8.0 / jnp.maximum(largest, 1e-30)


def coded(value, scale):
    base = jnp.abs(value) * scale + 8.0 * OFFSET
    two = base * base
    four = two * two
    eight = four * four
    sixteen = eight * eight
    power = sixteen * sixteen * eight
    return jnp.where(value < 0.0, -power, power)


def decoded(code, largest):
    root = jnp.exp2(jnp.log2(jnp.abs(code)) * (1.0 / 40.0))
    size = root * (largest * 0.125) - largest * OFFSET
    return jnp.where(code < 0.0, -size, size)


def kernel(
    filt_hbm, proj_hbm, taps_hbm, grad_hbm, first_hbm, second_hbm, twist_hbm, back_hbm, last_hbm,
    mixed, grad_streams, grad_filter,
    filt, proj, taps, grad, first, second, twist, back, last,
    sent, got, made, home, scales_out, scales_in, plain, gathered, results, streams, halo, spectra,
    load_sem, send_sem, recv_sem, halo_sem,
):
    loads = [
        pltpu.make_async_copy(source, target, load_sem.at[i])
        for i, (source, target) in enumerate((
            (filt_hbm, filt), (proj_hbm, proj), (taps_hbm, taps), (grad_hbm, grad), (first_hbm, first),
            (second_hbm, second), (twist_hbm, twist), (back_hbm, back), (last_hbm, last),
        ))
    ]
    for load in loads:
        load.start()
    me = lax.axis_index("ctx")
    row, column = me // 4, me % 4

    def peer_of(step):
        return (row + step // 4) % 4 * 4 + (column + step % 4) % 4

    peers = [peer_of(step) for step in range(1, DEVICES)]

    def each_peer(action):
        for peer in peers:
            action(peer)

    pairs = [(sent.at[m], got.at[m]) for m in range(3)] + [(made.at[m], home.at[m]) for m in range(3)]
    pairs += [(scales_out.at[m], scales_in.at[m]) for m in range(6)]

    def copy_to(message, peer):
        source, target = pairs[message]
        return pltpu.make_async_remote_copy(
            src_ref=source.at[peer], dst_ref=target.at[me],
            send_sem=send_sem.at[message], recv_sem=recv_sem.at[message],
            device_id={"ctx": peer}, device_id_type=MESH,
        )

    def all_copies(message):
        source, target = pairs[message]
        every = pl.ds(0, DEVICES - 1)
        return pltpu.make_async_remote_copy(
            src_ref=source.at[every], dst_ref=target.at[every],
            send_sem=send_sem.at[message], recv_sem=recv_sem.at[message],
            device_id={"ctx": peers[0]}, device_id_type=MESH,
        )

    def send(message):
        def start(peer):
            copy_to(message + 6, peer).start()
            copy_to(message, peer).start()
        each_peer(start)
        for source, target in (pairs[message], pairs[message + 6]):
            target[me] = source[me]

    def receive(message):
        all_copies(message + 6).wait_recv()
        all_copies(message).wait_recv()

    def rows_of(block):
        return pl.ds(pl.multiple_of(block * SIDE, SIDE), SIDE)

    def code_rows(pair):
        return pl.ds(pl.multiple_of(pair * 2 * SUB, 2 * SUB), 2 * SUB)

    def turned_out(message, source):
        largest = jnp.max(jnp.abs(source[...]), axis=0, keepdims=True)
        scales_out[message] = jnp.broadcast_to(largest[None], (DEVICES, 1, SIDE))
        scale = scale_of(largest)

        def body(pair, carry):
            turned = [
                coded(source[rows_of(2 * pair + i), :], scale).T.reshape(DEVICES, SUB, SIDE) for i in range(2)
            ]
            sent[message, :, code_rows(pair), :] = jnp.concatenate(turned, axis=1).astype(BF16)
            return carry
        lax.fori_loop(0, BLOCKS // 2, body, 0)

    barrier = pltpu.get_barrier_semaphore()
    each_peer(lambda peer: pl.semaphore_signal(barrier, inc=1, device_id={"ctx": peer}, device_id_type=MESH))
    loads[0].wait()
    turned_out(0, filt)
    pl.semaphore_wait(barrier, DEVICES - 1)
    loads[1].wait()
    after, before = (me + 1) % DEVICES, (me + DEVICES - 1) % DEVICES
    tail = pl.ds(BLOCKS * SIDE - 16, 16)

    def halo_copy(peer):
        return pltpu.make_async_remote_copy(
            src_ref=proj.at[:, tail, :], dst_ref=halo, send_sem=halo_sem.at[0], recv_sem=halo_sem.at[1],
            device_id={"ctx": peer}, device_id_type=MESH,
        )

    halo_copy(after).start()
    send(0)

    def short(stream, block, previous):
        now = proj[stream, rows_of(block), :].astype(F32)
        window = jnp.concatenate([previous[8:], now], axis=0)
        value = (
            taps[stream, 0:1, :] * now
            + taps[stream, 1:2, :] * window[7 : 7 + SIDE]
            + taps[stream, 2:3, :] * window[6 : 6 + SIDE]
        )
        streams[stream, rows_of(block), :] = value
        return value

    def inside(stream, block):
        return proj[stream, pl.ds(pl.multiple_of(block * SIDE - 16, 16), 16), :].astype(F32)

    def edge(stream):
        return jnp.where(me > 0, halo[stream].astype(F32), 0.0)

    def key_value(block, previous):
        plain[rows_of(block), :] = short(1, block, previous(1)) * short(2, block, previous(2))

    def back_gated(block, previous):
        plain[rows_of(block), :] = short(0, block, previous(0)) * grad[rows_of(block), :].astype(F32)

    def later_blocks(make):
        def body(block, carry):
            make(block, lambda stream: inside(stream, block))
            return carry
        lax.fori_loop(1, BLOCKS, body, 0)

    loads[2].wait()
    later_blocks(key_value)
    halo_copy(before).wait_recv()
    key_value(0, edge)
    turned_out(1, plain)
    send(1)
    loads[3].wait()
    later_blocks(back_gated)
    back_gated(0, edge)
    turned_out(2, plain)
    send(2)

    def lane_is_own(shape, axis):
        lane = lax.broadcasted_iota(jnp.int32, shape, len(shape) - 1)
        return lane == SUB * me + lax.broadcasted_iota(jnp.int32, shape, axis)

    def gather(message):
        receive(message)
        shape = (DEVICES, SUB, SIDE)
        rows = jnp.broadcast_to(scales_in[message], shape)
        largest = jnp.sum(jnp.where(lane_is_own(shape, 1), rows, 0.0), axis=2, keepdims=True)
        for source in range(DEVICES):
            code = got[message, source].astype(F32).reshape(BLOCKS, SUB, SIDE)
            gathered[source] = decoded(code, largest[source : source + 1]).reshape(BLOCKS * SUB, SIDE)

    def scatter(message):
        for target in range(DEVICES):
            value = results[target].reshape(BLOCKS, SUB, SIDE)
            largest = jnp.max(jnp.max(jnp.abs(value), axis=0), axis=1, keepdims=True)
            spread = jnp.where(lane_is_own((SUB, SIDE), 0), largest, 0.0)
            scales_out[message, target] = jnp.sum(spread, axis=0, keepdims=True)
            made[message - 3, target] = coded(value, scale_of(largest)[None]).reshape(BLOCKS * SUB, SIDE).astype(BF16)
        send(message)

    def forward(pair):
        parts = [gathered[:, pl.ds(2 * pair + i, SUB, stride=SUB), :].reshape(SIDE, SIDE) for i in range(2)]
        mixed_rows = left_product(first, jnp.concatenate(parts, axis=1))
        cos, sin = twist[0], twist[1]
        rows = []
        for i in range(2):
            real = mixed_rows[:SIDE, i * SIDE : (i + 1) * SIDE]
            imag = mixed_rows[SIDE:, i * SIDE : (i + 1) * SIDE]
            rows.append(jnp.concatenate([real * cos + imag * sin, imag * cos - real * sin], axis=1))
        return right_product(jnp.concatenate(rows, axis=0), second)

    def inverse(pair, real, imag):
        value = right_product(jnp.concatenate([real, imag], axis=1), back)
        cos, sin = twist[0], twist[1]
        columns = []
        for i in range(2):
            real = value[i * SIDE : (i + 1) * SIDE, :SIDE]
            imag = value[i * SIDE : (i + 1) * SIDE, SIDE:]
            columns.append(jnp.concatenate([real * cos - imag * sin, real * sin + imag * cos], axis=0))
        result = left_product(last, jnp.concatenate(columns, axis=1))
        for i in range(2):
            results[:, pl.ds(2 * pair + i, SUB, stride=SUB), :] = result[:, i * SIDE : (i + 1) * SIDE].reshape(
                DEVICES, SUB, SIDE
            )

    def parts_of(value):
        return value[:, :SIDE], value[:, SIDE:]

    def each_pair(action):
        for pair in range(SUB // 2):
            action(pair)

    def spectrum(signal):
        def action(pair):
            spectra[signal, pair] = forward(pair)
        each_pair(action)

    def conv_pair(pair):
        (fr, fi), (vr, vi) = parts_of(spectra[0, pair]), parts_of(spectra[1, pair])
        inverse(pair, fr * vr - fi * vi, fr * vi + fi * vr)

    def stream_pair(pair):
        (fr, fi), (br, bi) = parts_of(spectra[0, pair]), parts_of(spectra[2, pair])
        inverse(pair, fr * br + fi * bi, fr * bi - fi * br)

    def filt_pair(pair):
        (vr, vi), (br, bi) = parts_of(spectra[1, pair]), parts_of(spectra[2, pair])
        inverse(pair, vr * br + vi * bi, vr * bi - vi * br)

    for load in loads[4:]:
        load.wait()
    gather(0)
    spectrum(0)
    gather(1)
    spectrum(1)
    each_pair(conv_pair)
    scatter(3)
    gather(2)
    spectrum(2)
    each_pair(stream_pair)
    scatter(4)
    each_pair(filt_pair)
    scatter(5)

    def turned_home(message, action):
        receive(message)
        largest = jnp.sum(scales_in[message], axis=0)

        def body(pair, carry):
            code = home[message - 3, :, code_rows(pair), :].astype(F32)
            for i in range(2):
                turned = code[:, i * SUB : (i + 1) * SUB, :].reshape(SIDE, SIDE).T
                action(rows_of(2 * pair + i), decoded(turned, largest))
            return carry
        lax.fori_loop(0, BLOCKS // 2, body, 0)

    def conv_home(rows, value):
        mixed[rows, :] = (streams[0, rows, :] * value).astype(BF16)
        grad_streams[0, rows, :] = (grad[rows, :].astype(F32) * value).astype(BF16)

    def stream_home(rows, value):
        grad_streams[1, rows, :] = (value * streams[2, rows, :]).astype(BF16)
        grad_streams[2, rows, :] = (value * streams[1, rows, :]).astype(BF16)

    def filt_home(rows, value):
        grad_filter[rows, :] = value * (1.0 / SIDE)

    turned_home(3, conv_home)
    turned_home(4, stream_home)
    turned_home(5, filt_home)
    for message in range(12):
        all_copies(message).wait_send()
    halo_copy(after).wait_send()


def write_out(mixed, grad_streams, grad_filter, mixed_hbm, grad_streams_hbm, grad_filter_hbm, sems):
    copies = [
        pltpu.make_async_copy(source, target, sems.at[i])
        for i, (source, target) in enumerate((
            (grad_streams, grad_streams_hbm), (grad_filter, grad_filter_hbm), (mixed, mixed_hbm),
        ))
    ]
    for copy in copies:
        copy.start()
    for copy in copies:
        copy.wait()


def local(projected, short_taps, long_filter, grad_mixed):
    first, second, back, last, twist = (jnp.asarray(table) for table in tables())
    operands = (long_filter, projected, short_taps, grad_mixed, first, second, twist, back, last)
    tokens, channels = grad_mixed.shape
    in_vmem = pl.BlockSpec(memory_space=pltpu.VMEM)
    in_hbm = pl.BlockSpec(memory_space=pltpu.MemorySpace.HBM)
    buffer = pltpu.VMEM((3, DEVICES, SUB * BLOCKS, SIDE), BF16)
    scales = pltpu.VMEM((6, DEVICES, 1, SIDE), F32)
    whole = pltpu.VMEM((DEVICES, SUB * BLOCKS, SIDE), F32)
    out_shape = (
        jax.ShapeDtypeStruct((tokens, channels), BF16),
        jax.ShapeDtypeStruct((3, tokens, channels), BF16),
        jax.ShapeDtypeStruct((tokens, channels), F32),
    )
    results = pl.pallas_call(
        kernel,
        out_shape=out_shape,
        in_specs=[in_hbm] * len(operands),
        out_specs=(in_vmem,) * 3,
        scratch_shapes=[pltpu.VMEM(operand.shape, operand.dtype) for operand in operands]
        + [
            buffer, buffer, buffer, buffer, scales, scales,
            pltpu.VMEM((tokens, channels), F32), whole, whole,
            pltpu.VMEM((3, tokens, channels), F32),
            pltpu.VMEM((3, 16, channels), BF16),
            pltpu.VMEM((3, SUB // 2, 2 * SIDE, 2 * SIDE), F32),
            pltpu.SemaphoreType.DMA((len(operands),)),
            pltpu.SemaphoreType.DMA((12,)),
            pltpu.SemaphoreType.DMA((12,)),
            pltpu.SemaphoreType.DMA((2,)),
        ],
        compiler_params=pltpu.CompilerParams(
            collective_id=0, has_side_effects=True, vmem_limit_bytes=40 * 1024 * 1024
        ),
    )(*[pltpu.with_memory_space_constraint(operand, pltpu.MemorySpace.HBM) for operand in operands])
    return pl.pallas_call(
        write_out,
        out_shape=out_shape,
        in_specs=[in_vmem] * 3,
        out_specs=(in_hbm,) * 3,
        scratch_shapes=[pltpu.SemaphoreType.DMA((3,))],
    )(*[pltpu.with_memory_space_constraint(result, pltpu.VMEM) for result in results])


def solution(mesh):
    in_specs = (P(None, "ctx", "ch"), P(None, None, "ch"), P("ctx", "ch"), P("ctx", "ch"))
    out_specs = (P("ctx", "ch"), P(None, "ctx", "ch"), P("ctx", "ch"))
    return jax.shard_map(local, mesh=mesh, in_specs=in_specs, out_specs=out_specs, check_vma=False)
```

```python
import math

import jax
import jax.numpy as jnp
import ml_dtypes
import numpy as np
from jax import lax
from jax.experimental import pallas as pl
from jax.experimental.pallas import tpu as pltpu
from jax.sharding import PartitionSpec as P

MESH = pl.DeviceIdType.MESH
SIDE = 128
DEVICES = 16
SUB = 8
BLOCKS = 8
OFFSET = 1.0 / 64.0
F32, BF16 = jnp.float32, jnp.bfloat16


def halves(table):
    high = table.astype(ml_dtypes.bfloat16)
    low = (table - high.astype(np.float64)).astype(ml_dtypes.bfloat16)
    return high, low


def along(table, axis):
    high, low = halves(table)
    return np.concatenate([high, high, low], axis=axis)


def tables():
    index = np.arange(SIDE)
    outer = 2.0 * math.pi * ((4 * index[:, None] + 1) * index[None, :] % (4 * SIDE)) / (4 * SIDE)
    inner = 2.0 * math.pi * (index[:, None] * index[None, :] % SIDE) / SIDE
    turn = 2.0 * math.pi * ((4 * index[:, None] + 1) * index[None, :]) / (4 * SIDE * SIDE)
    first = np.concatenate([np.cos(outer), -np.sin(outer)], axis=0)
    cos, sin = np.cos(inner), np.sin(inner)
    second = np.block([[cos, -sin], [sin, cos]])
    back = np.block([[cos, sin], [-sin, cos]])
    last = np.concatenate([np.cos(outer).T, -np.sin(outer).T], axis=1) / (SIDE * SIDE)
    twist = np.stack([np.cos(turn), np.sin(turn)]).astype(np.float32)
    return along(first, 1), along(second, 0), along(back, 0), along(last, 1), twist


def split(value):
    high = value.astype(BF16)
    return high, (value - high.astype(F32)).astype(BF16)


def dot(left, right):
    return jnp.dot(left, right, preferred_element_type=F32)


def left_product(table, value):
    high, low = split(value)
    return dot(table[...], jnp.concatenate([high, low, high], axis=0))


def right_product(value, table):
    high, low = split(value)
    return dot(jnp.concatenate([high, low, high], axis=1), table[...])


def scale_of(largest):
    return 8.0 / jnp.maximum(largest, 1e-30)


def coded(value, scale):
    base = jnp.abs(value) * scale + 8.0 * OFFSET
    two = base * base
    four = two * two
    eight = four * four
    sixteen = eight * eight
    power = sixteen * sixteen * eight
    return jnp.where(value < 0.0, -power, power)


def decoded(code, largest):
    root = jnp.exp2(jnp.log2(jnp.abs(code)) * (1.0 / 40.0))
    size = root * (largest * 0.125) - largest * OFFSET
    return jnp.where(code < 0.0, -size, size)


def kernel(
    filt_hbm, proj_hbm, taps_hbm, grad_hbm, first_hbm, second_hbm, twist_hbm, back_hbm, last_hbm,
    mixed, grad_streams, grad_filter,
    filt, proj, taps, grad, first, second, twist, back, last,
    sent, got, made, home, scales_out, scales_in, plain, gathered, results, streams, halo, spectra,
    load_sem, send_sem, recv_sem, halo_sem,
):
    loads = [
        pltpu.make_async_copy(source, target, load_sem.at[i])
        for i, (source, target) in enumerate((
            (filt_hbm, filt), (proj_hbm, proj), (taps_hbm, taps), (grad_hbm, grad), (first_hbm, first),
            (second_hbm, second), (twist_hbm, twist), (back_hbm, back), (last_hbm, last),
        ))
    ]
    for load in loads:
        load.start()
    me = lax.axis_index("ctx")
    row, column = me // 4, me % 4

    def peer_of(step):
        return (row + step // 4) % 4 * 4 + (column + step % 4) % 4

    def hops(step):
        return min(step // 4, 4 - step // 4) + min(step % 4, 4 - step % 4)

    peers = [peer_of(step) for step in sorted(range(1, DEVICES), key=hops, reverse=True)]

    def each_peer(action):
        for peer in peers:
            action(peer)

    pairs = [(sent.at[m], got.at[m]) for m in range(3)] + [(made.at[m], home.at[m]) for m in range(3)]
    pairs += [(scales_out.at[m], scales_in.at[m]) for m in range(6)]

    def copy_to(message, peer):
        source, target = pairs[message]
        return pltpu.make_async_remote_copy(
            src_ref=source.at[peer], dst_ref=target.at[me],
            send_sem=send_sem.at[message], recv_sem=recv_sem.at[message],
            device_id={"ctx": peer}, device_id_type=MESH,
        )

    def all_copies(message):
        source, target = pairs[message]
        every = pl.ds(0, DEVICES - 1)
        return pltpu.make_async_remote_copy(
            src_ref=source.at[every], dst_ref=target.at[every],
            send_sem=send_sem.at[message], recv_sem=recv_sem.at[message],
            device_id={"ctx": peers[0]}, device_id_type=MESH,
        )

    def send(message):
        def start(peer):
            copy_to(message + 6, peer).start()
            copy_to(message, peer).start()
        each_peer(start)
        for source, target in (pairs[message], pairs[message + 6]):
            target[me] = source[me]

    def receive(message):
        all_copies(message + 6).wait_recv()
        all_copies(message).wait_recv()

    def rows_of(block):
        return pl.ds(pl.multiple_of(block * SIDE, SIDE), SIDE)

    def code_rows(pair):
        return pl.ds(pl.multiple_of(pair * 2 * SUB, 2 * SUB), 2 * SUB)

    def turned_out(message, source):
        largest = jnp.max(jnp.abs(source[...]), axis=0, keepdims=True)
        scales_out[message] = jnp.broadcast_to(largest[None], (DEVICES, 1, SIDE))
        scale = scale_of(largest)

        def body(pair, carry):
            turned = [
                coded(source[rows_of(2 * pair + i), :], scale).T.reshape(DEVICES, SUB, SIDE) for i in range(2)
            ]
            sent[message, :, code_rows(pair), :] = jnp.concatenate(turned, axis=1).astype(BF16)
            return carry
        lax.fori_loop(0, BLOCKS // 2, body, 0)

    barrier = pltpu.get_barrier_semaphore()
    each_peer(lambda peer: pl.semaphore_signal(barrier, inc=1, device_id={"ctx": peer}, device_id_type=MESH))
    loads[0].wait()
    turned_out(0, filt)
    pl.semaphore_wait(barrier, DEVICES - 1)
    loads[1].wait()
    after, before = (me + 1) % DEVICES, (me + DEVICES - 1) % DEVICES
    tail = pl.ds(BLOCKS * SIDE - 16, 16)

    def halo_copy(peer):
        return pltpu.make_async_remote_copy(
            src_ref=proj.at[:, tail, :], dst_ref=halo, send_sem=halo_sem.at[0], recv_sem=halo_sem.at[1],
            device_id={"ctx": peer}, device_id_type=MESH,
        )

    halo_copy(after).start()
    send(0)

    def short(stream, block, previous):
        now = proj[stream, rows_of(block), :].astype(F32)
        window = jnp.concatenate([previous[8:], now], axis=0)
        value = (
            taps[stream, 0:1, :] * now
            + taps[stream, 1:2, :] * window[7 : 7 + SIDE]
            + taps[stream, 2:3, :] * window[6 : 6 + SIDE]
        )
        streams[stream, rows_of(block), :] = value
        return value

    def inside(stream, block):
        return proj[stream, pl.ds(pl.multiple_of(block * SIDE - 16, 16), 16), :].astype(F32)

    def edge(stream):
        return jnp.where(me > 0, halo[stream].astype(F32), 0.0)

    def key_value(block, previous):
        plain[rows_of(block), :] = short(1, block, previous(1)) * short(2, block, previous(2))

    def back_gated(block, previous):
        plain[rows_of(block), :] = short(0, block, previous(0)) * grad[rows_of(block), :].astype(F32)

    def later_blocks(make):
        def body(block, carry):
            make(block, lambda stream: inside(stream, block))
            return carry
        lax.fori_loop(1, BLOCKS, body, 0)

    loads[2].wait()
    later_blocks(key_value)
    halo_copy(before).wait_recv()
    key_value(0, edge)
    turned_out(1, plain)
    send(1)
    loads[3].wait()
    later_blocks(back_gated)
    back_gated(0, edge)
    turned_out(2, plain)
    send(2)

    def lane_is_own(shape, axis):
        lane = lax.broadcasted_iota(jnp.int32, shape, len(shape) - 1)
        return lane == SUB * me + lax.broadcasted_iota(jnp.int32, shape, axis)

    def gather(message):
        receive(message)
        shape = (DEVICES, SUB, SIDE)
        rows = jnp.broadcast_to(scales_in[message], shape)
        largest = jnp.sum(jnp.where(lane_is_own(shape, 1), rows, 0.0), axis=2, keepdims=True)
        for source in range(DEVICES):
            code = got[message, source].astype(F32).reshape(BLOCKS, SUB, SIDE)
            gathered[source] = decoded(code, largest[source : source + 1]).reshape(BLOCKS * SUB, SIDE)

    def scatter(message):
        for target in range(DEVICES):
            value = results[target].reshape(BLOCKS, SUB, SIDE)
            largest = jnp.max(jnp.max(jnp.abs(value), axis=0), axis=1, keepdims=True)
            spread = jnp.where(lane_is_own((SUB, SIDE), 0), largest, 0.0)
            scales_out[message, target] = jnp.sum(spread, axis=0, keepdims=True)
            made[message - 3, target] = coded(value, scale_of(largest)[None]).reshape(BLOCKS * SUB, SIDE).astype(BF16)
        send(message)

    def forward(pair):
        parts = [gathered[:, pl.ds(2 * pair + i, SUB, stride=SUB), :].reshape(SIDE, SIDE) for i in range(2)]
        mixed_rows = left_product(first, jnp.concatenate(parts, axis=1))
        cos, sin = twist[0], twist[1]
        rows = []
        for i in range(2):
            real = mixed_rows[:SIDE, i * SIDE : (i + 1) * SIDE]
            imag = mixed_rows[SIDE:, i * SIDE : (i + 1) * SIDE]
            rows.append(jnp.concatenate([real * cos + imag * sin, imag * cos - real * sin], axis=1))
        return right_product(jnp.concatenate(rows, axis=0), second)

    def inverse(pair, real, imag):
        value = right_product(jnp.concatenate([real, imag], axis=1), back)
        cos, sin = twist[0], twist[1]
        columns = []
        for i in range(2):
            real = value[i * SIDE : (i + 1) * SIDE, :SIDE]
            imag = value[i * SIDE : (i + 1) * SIDE, SIDE:]
            columns.append(jnp.concatenate([real * cos - imag * sin, real * sin + imag * cos], axis=0))
        result = left_product(last, jnp.concatenate(columns, axis=1))
        for i in range(2):
            results[:, pl.ds(2 * pair + i, SUB, stride=SUB), :] = result[:, i * SIDE : (i + 1) * SIDE].reshape(
                DEVICES, SUB, SIDE
            )

    def parts_of(value):
        return value[:, :SIDE], value[:, SIDE:]

    def each_pair(action):
        for pair in range(SUB // 2):
            action(pair)

    def spectrum(signal):
        def action(pair):
            spectra[signal, pair] = forward(pair)
        each_pair(action)

    def conv_pair(pair):
        (fr, fi), (vr, vi) = parts_of(spectra[0, pair]), parts_of(spectra[1, pair])
        inverse(pair, fr * vr - fi * vi, fr * vi + fi * vr)

    def stream_pair(pair):
        (fr, fi), (br, bi) = parts_of(spectra[0, pair]), parts_of(spectra[2, pair])
        inverse(pair, fr * br + fi * bi, fr * bi - fi * br)

    def filt_pair(pair):
        (vr, vi), (br, bi) = parts_of(spectra[1, pair]), parts_of(spectra[2, pair])
        inverse(pair, vr * br + vi * bi, vr * bi - vi * br)

    for load in loads[4:]:
        load.wait()
    gather(0)
    spectrum(0)
    gather(1)
    spectrum(1)
    each_pair(conv_pair)
    scatter(3)
    gather(2)
    spectrum(2)
    each_pair(stream_pair)
    scatter(4)
    each_pair(filt_pair)
    scatter(5)

    def turned_home(message, action):
        receive(message)
        largest = jnp.sum(scales_in[message], axis=0)

        def body(pair, carry):
            code = home[message - 3, :, code_rows(pair), :].astype(F32)
            for i in range(2):
                turned = code[:, i * SUB : (i + 1) * SUB, :].reshape(SIDE, SIDE).T
                action(rows_of(2 * pair + i), decoded(turned, largest))
            return carry
        lax.fori_loop(0, BLOCKS // 2, body, 0)

    def conv_home(rows, value):
        mixed[rows, :] = (streams[0, rows, :] * value).astype(BF16)
        grad_streams[0, rows, :] = (grad[rows, :].astype(F32) * value).astype(BF16)

    def stream_home(rows, value):
        grad_streams[1, rows, :] = (value * streams[2, rows, :]).astype(BF16)
        grad_streams[2, rows, :] = (value * streams[1, rows, :]).astype(BF16)

    def filt_home(rows, value):
        grad_filter[rows, :] = value * (1.0 / SIDE)

    turned_home(3, conv_home)
    turned_home(4, stream_home)
    turned_home(5, filt_home)
    for message in range(12):
        all_copies(message).wait_send()
    halo_copy(after).wait_send()


def write_out(mixed, grad_streams, grad_filter, mixed_hbm, grad_streams_hbm, grad_filter_hbm, sems):
    copies = [
        pltpu.make_async_copy(source, target, sems.at[i])
        for i, (source, target) in enumerate((
            (grad_streams, grad_streams_hbm), (grad_filter, grad_filter_hbm), (mixed, mixed_hbm),
        ))
    ]
    for copy in copies:
        copy.start()
    for copy in copies:
        copy.wait()


def local(projected, short_taps, long_filter, grad_mixed):
    first, second, back, last, twist = (jnp.asarray(table) for table in tables())
    operands = (long_filter, projected, short_taps, grad_mixed, first, second, twist, back, last)
    tokens, channels = grad_mixed.shape
    in_vmem = pl.BlockSpec(memory_space=pltpu.VMEM)
    in_hbm = pl.BlockSpec(memory_space=pltpu.MemorySpace.HBM)
    buffer = pltpu.VMEM((3, DEVICES, SUB * BLOCKS, SIDE), BF16)
    scales = pltpu.VMEM((6, DEVICES, 1, SIDE), F32)
    whole = pltpu.VMEM((DEVICES, SUB * BLOCKS, SIDE), F32)
    out_shape = (
        jax.ShapeDtypeStruct((tokens, channels), BF16),
        jax.ShapeDtypeStruct((3, tokens, channels), BF16),
        jax.ShapeDtypeStruct((tokens, channels), F32),
    )
    results = pl.pallas_call(
        kernel,
        out_shape=out_shape,
        in_specs=[in_hbm] * len(operands),
        out_specs=(in_vmem,) * 3,
        scratch_shapes=[pltpu.VMEM(operand.shape, operand.dtype) for operand in operands]
        + [
            buffer, buffer, buffer, buffer, scales, scales,
            pltpu.VMEM((tokens, channels), F32), whole, whole,
            pltpu.VMEM((3, tokens, channels), F32),
            pltpu.VMEM((3, 16, channels), BF16),
            pltpu.VMEM((3, SUB // 2, 2 * SIDE, 2 * SIDE), F32),
            pltpu.SemaphoreType.DMA((len(operands),)),
            pltpu.SemaphoreType.DMA((12,)),
            pltpu.SemaphoreType.DMA((12,)),
            pltpu.SemaphoreType.DMA((2,)),
        ],
        compiler_params=pltpu.CompilerParams(
            collective_id=0, has_side_effects=True, vmem_limit_bytes=40 * 1024 * 1024
        ),
    )(*[pltpu.with_memory_space_constraint(operand, pltpu.MemorySpace.HBM) for operand in operands])
    return pl.pallas_call(
        write_out,
        out_shape=out_shape,
        in_specs=[in_vmem] * 3,
        out_specs=(in_hbm,) * 3,
        scratch_shapes=[pltpu.SemaphoreType.DMA((3,))],
    )(*[pltpu.with_memory_space_constraint(result, pltpu.VMEM) for result in results])


def solution(mesh):
    in_specs = (P(None, "ctx", "ch"), P(None, None, "ch"), P("ctx", "ch"), P("ctx", "ch"))
    out_specs = (P("ctx", "ch"), P(None, "ctx", "ch"), P("ctx", "ch"))
    return jax.shard_map(local, mesh=mesh, in_specs=in_specs, out_specs=out_specs, check_vma=False)
```

```python
import math

import jax
import jax.numpy as jnp
import ml_dtypes
import numpy as np
from jax import lax
from jax.experimental import pallas as pl
from jax.experimental.pallas import tpu as pltpu
from jax.sharding import PartitionSpec as P

MESH = pl.DeviceIdType.MESH
SIDE = 128
DEVICES = 16
SUB = 8
GROUP = 4
BLOCKS = 8
OFFSET = 1.0 / 64.0
F32, BF16 = jnp.float32, jnp.bfloat16


def halves(table):
    high = table.astype(ml_dtypes.bfloat16)
    low = (table - high.astype(np.float64)).astype(ml_dtypes.bfloat16)
    return high, low


def along(table, axis):
    high, low = halves(table)
    return np.concatenate([high, high, low], axis=axis)


def tables():
    index = np.arange(SIDE)
    outer = 2.0 * math.pi * ((4 * index[:, None] + 1) * index[None, :] % (4 * SIDE)) / (4 * SIDE)
    inner = 2.0 * math.pi * (index[:, None] * index[None, :] % SIDE) / SIDE
    turn = 2.0 * math.pi * ((4 * index[:, None] + 1) * index[None, :]) / (4 * SIDE * SIDE)
    first = np.concatenate([np.cos(outer), -np.sin(outer)], axis=0)
    cos, sin = np.cos(inner), np.sin(inner)
    second = np.block([[cos, -sin], [sin, cos]])
    back = np.block([[cos, sin], [-sin, cos]])
    last = np.concatenate([np.cos(outer).T, -np.sin(outer).T], axis=1) / (SIDE * SIDE)
    twist = np.stack([np.cos(turn), np.sin(turn)]).astype(np.float32)
    return along(first, 1), along(second, 0), along(back, 0), along(last, 1), twist


def split(value):
    high = value.astype(BF16)
    return high, (value - high.astype(F32)).astype(BF16)


def dot(left, right):
    return jnp.dot(left, right, preferred_element_type=F32)


def left_product(table, value):
    high, low = split(value)
    return dot(table[...], jnp.concatenate([high, low, high], axis=0))


def right_product(value, table):
    high, low = split(value)
    return dot(jnp.concatenate([high, low, high], axis=1), table[...])


def scale_of(largest):
    return 8.0 / jnp.maximum(largest, 1e-30)


def coded(value, scale):
    base = jnp.abs(value) * scale + 8.0 * OFFSET
    two = base * base
    four = two * two
    eight = four * four
    sixteen = eight * eight
    power = sixteen * sixteen * eight
    return jnp.where(value < 0.0, -power, power)


def decoded(code, largest):
    root = jnp.exp2(jnp.log2(jnp.abs(code)) * (1.0 / 40.0))
    size = root * (largest * 0.125) - largest * OFFSET
    return jnp.where(code < 0.0, -size, size)


def kernel(
    filt_hbm, proj_hbm, taps_hbm, grad_hbm, first_hbm, second_hbm, twist_hbm, back_hbm, last_hbm,
    mixed, grad_streams, grad_filter,
    filt, proj, taps, grad, first, second, twist, back, last,
    sent, got, made, home, scales_out, scales_in, plain, gathered, results, streams, halo, spectra,
    load_sem, send_sem, recv_sem, halo_sem,
):
    loads = [
        pltpu.make_async_copy(source, target, load_sem.at[i])
        for i, (source, target) in enumerate((
            (filt_hbm, filt), (proj_hbm, proj), (taps_hbm, taps), (grad_hbm, grad), (first_hbm, first),
            (second_hbm, second), (twist_hbm, twist), (back_hbm, back), (last_hbm, last),
        ))
    ]
    for load in loads:
        load.start()
    me = lax.axis_index("ctx")
    row, column = me // 4, me % 4

    def peer_of(step):
        return (row + step // 4) % 4 * 4 + (column + step % 4) % 4

    def hops(step):
        return min(step // 4, 4 - step // 4) + min(step % 4, 4 - step % 4)

    peers = [peer_of(step) for step in sorted(range(1, DEVICES), key=hops, reverse=True)]

    def each_peer(action):
        for peer in peers:
            action(peer)

    pairs = [(sent.at[m], got.at[m]) for m in range(3)] + [(made.at[m], home.at[m]) for m in range(3)]
    pairs += [(scales_out.at[m], scales_in.at[m]) for m in range(6)]

    def copy_to(message, peer):
        source, target = pairs[message]
        return pltpu.make_async_remote_copy(
            src_ref=source.at[peer], dst_ref=target.at[me],
            send_sem=send_sem.at[message], recv_sem=recv_sem.at[message],
            device_id={"ctx": peer}, device_id_type=MESH,
        )

    def all_copies(message):
        source, target = pairs[message]
        every = pl.ds(0, DEVICES - 1)
        return pltpu.make_async_remote_copy(
            src_ref=source.at[every], dst_ref=target.at[every],
            send_sem=send_sem.at[message], recv_sem=recv_sem.at[message],
            device_id={"ctx": peers[0]}, device_id_type=MESH,
        )

    def send(message):
        def start(peer):
            copy_to(message + 6, peer).start()
            copy_to(message, peer).start()
        each_peer(start)
        for source, target in (pairs[message], pairs[message + 6]):
            target[me] = source[me]

    def receive(message):
        all_copies(message + 6).wait_recv()
        all_copies(message).wait_recv()

    def rows_of(block):
        return pl.ds(pl.multiple_of(block * SIDE, SIDE), SIDE)

    def code_rows(pair):
        return pl.ds(pl.multiple_of(pair * 2 * SUB, 2 * SUB), 2 * SUB)

    def turned_out(message, source):
        largest = jnp.max(jnp.abs(source[...]), axis=0, keepdims=True)
        scales_out[message] = jnp.broadcast_to(largest[None], (DEVICES, 1, SIDE))
        scale = scale_of(largest)

        def body(pair, carry):
            turned = [
                coded(source[rows_of(2 * pair + i), :], scale).T.reshape(DEVICES, SUB, SIDE) for i in range(2)
            ]
            sent[message, :, code_rows(pair), :] = jnp.concatenate(turned, axis=1).astype(BF16)
            return carry
        lax.fori_loop(0, BLOCKS // 2, body, 0)

    barrier = pltpu.get_barrier_semaphore()
    each_peer(lambda peer: pl.semaphore_signal(barrier, inc=1, device_id={"ctx": peer}, device_id_type=MESH))
    loads[0].wait()
    turned_out(0, filt)
    pl.semaphore_wait(barrier, DEVICES - 1)
    loads[1].wait()
    after, before = (me + 1) % DEVICES, (me + DEVICES - 1) % DEVICES
    tail = pl.ds(BLOCKS * SIDE - 16, 16)

    def halo_copy(peer):
        return pltpu.make_async_remote_copy(
            src_ref=proj.at[:, tail, :], dst_ref=halo, send_sem=halo_sem.at[0], recv_sem=halo_sem.at[1],
            device_id={"ctx": peer}, device_id_type=MESH,
        )

    halo_copy(after).start()
    send(0)

    def short(stream, block, previous):
        now = proj[stream, rows_of(block), :].astype(F32)
        window = jnp.concatenate([previous[8:], now], axis=0)
        value = (
            taps[stream, 0:1, :] * now
            + taps[stream, 1:2, :] * window[7 : 7 + SIDE]
            + taps[stream, 2:3, :] * window[6 : 6 + SIDE]
        )
        streams[stream, rows_of(block), :] = value
        return value

    def inside(stream, block):
        return proj[stream, pl.ds(pl.multiple_of(block * SIDE - 16, 16), 16), :].astype(F32)

    def edge(stream):
        return jnp.where(me > 0, halo[stream].astype(F32), 0.0)

    def key_value(block, previous):
        plain[rows_of(block), :] = short(1, block, previous(1)) * short(2, block, previous(2))

    def back_gated(block, previous):
        plain[rows_of(block), :] = short(0, block, previous(0)) * grad[rows_of(block), :].astype(F32)

    def later_blocks(make):
        def body(block, carry):
            make(block, lambda stream: inside(stream, block))
            return carry
        lax.fori_loop(1, BLOCKS, body, 0)

    loads[2].wait()
    later_blocks(key_value)
    halo_copy(before).wait_recv()
    key_value(0, edge)
    turned_out(1, plain)
    send(1)
    loads[3].wait()
    later_blocks(back_gated)
    back_gated(0, edge)
    turned_out(2, plain)
    send(2)

    def lane_is_own(shape, axis):
        lane = lax.broadcasted_iota(jnp.int32, shape, len(shape) - 1)
        return lane == SUB * me + lax.broadcasted_iota(jnp.int32, shape, axis)

    def gather(message):
        receive(message)
        shape = (DEVICES, SUB, SIDE)
        rows = jnp.broadcast_to(scales_in[message], shape)
        largest = jnp.sum(jnp.where(lane_is_own(shape, 1), rows, 0.0), axis=2, keepdims=True)
        for source in range(DEVICES):
            code = got[message, source].astype(F32).reshape(BLOCKS, SUB, SIDE)
            gathered[source] = decoded(code, largest[source : source + 1]).reshape(BLOCKS * SUB, SIDE)

    def scatter(message):
        for target in range(DEVICES):
            value = results[target].reshape(BLOCKS, SUB, SIDE)
            largest = jnp.max(jnp.max(jnp.abs(value), axis=0), axis=1, keepdims=True)
            spread = jnp.where(lane_is_own((SUB, SIDE), 0), largest, 0.0)
            scales_out[message, target] = jnp.sum(spread, axis=0, keepdims=True)
            made[message - 3, target] = coded(value, scale_of(largest)[None]).reshape(BLOCKS * SUB, SIDE).astype(BF16)
        send(message)

    def forward(pair):
        parts = [gathered[:, pl.ds(GROUP * pair + i, SUB, stride=SUB), :].reshape(SIDE, SIDE) for i in range(GROUP)]
        mixed_rows = left_product(first, jnp.concatenate(parts, axis=1))
        cos, sin = twist[0], twist[1]
        rows = []
        for i in range(GROUP):
            real = mixed_rows[:SIDE, i * SIDE : (i + 1) * SIDE]
            imag = mixed_rows[SIDE:, i * SIDE : (i + 1) * SIDE]
            rows.append(jnp.concatenate([real * cos + imag * sin, imag * cos - real * sin], axis=1))
        return right_product(jnp.concatenate(rows, axis=0), second)

    def inverse(pair, real, imag):
        value = right_product(jnp.concatenate([real, imag], axis=1), back)
        cos, sin = twist[0], twist[1]
        columns = []
        for i in range(GROUP):
            real = value[i * SIDE : (i + 1) * SIDE, :SIDE]
            imag = value[i * SIDE : (i + 1) * SIDE, SIDE:]
            columns.append(jnp.concatenate([real * cos - imag * sin, real * sin + imag * cos], axis=0))
        result = left_product(last, jnp.concatenate(columns, axis=1))
        for i in range(GROUP):
            results[:, pl.ds(GROUP * pair + i, SUB, stride=SUB), :] = result[:, i * SIDE : (i + 1) * SIDE].reshape(
                DEVICES, SUB, SIDE
            )

    def parts_of(value):
        return value[:, :SIDE], value[:, SIDE:]

    def each_pair(action):
        for pair in range(SUB // GROUP):
            action(pair)

    def spectrum(signal):
        def action(pair):
            spectra[signal, pair] = forward(pair)
        each_pair(action)

    def conv_pair(pair):
        (fr, fi), (vr, vi) = parts_of(spectra[0, pair]), parts_of(spectra[1, pair])
        inverse(pair, fr * vr - fi * vi, fr * vi + fi * vr)

    def stream_pair(pair):
        (fr, fi), (br, bi) = parts_of(spectra[0, pair]), parts_of(spectra[2, pair])
        inverse(pair, fr * br + fi * bi, fr * bi - fi * br)

    def filt_pair(pair):
        (vr, vi), (br, bi) = parts_of(spectra[1, pair]), parts_of(spectra[2, pair])
        inverse(pair, vr * br + vi * bi, vr * bi - vi * br)

    for load in loads[4:]:
        load.wait()
    gather(0)
    spectrum(0)
    gather(1)
    spectrum(1)
    each_pair(conv_pair)
    scatter(3)
    gather(2)
    spectrum(2)
    each_pair(stream_pair)
    scatter(4)
    each_pair(filt_pair)
    scatter(5)

    def turned_home(message, action):
        receive(message)
        largest = jnp.sum(scales_in[message], axis=0)

        def body(pair, carry):
            code = home[message - 3, :, code_rows(pair), :].astype(F32)
            for i in range(2):
                turned = code[:, i * SUB : (i + 1) * SUB, :].reshape(SIDE, SIDE).T
                action(rows_of(2 * pair + i), decoded(turned, largest))
            return carry
        lax.fori_loop(0, BLOCKS // 2, body, 0)

    def conv_home(rows, value):
        mixed[rows, :] = (streams[0, rows, :] * value).astype(BF16)
        grad_streams[0, rows, :] = (grad[rows, :].astype(F32) * value).astype(BF16)

    def stream_home(rows, value):
        grad_streams[1, rows, :] = (value * streams[2, rows, :]).astype(BF16)
        grad_streams[2, rows, :] = (value * streams[1, rows, :]).astype(BF16)

    def filt_home(rows, value):
        grad_filter[rows, :] = value * (1.0 / SIDE)

    turned_home(3, conv_home)
    turned_home(4, stream_home)
    turned_home(5, filt_home)
    for message in range(12):
        all_copies(message).wait_send()
    halo_copy(after).wait_send()


def write_out(mixed, grad_streams, grad_filter, mixed_hbm, grad_streams_hbm, grad_filter_hbm, sems):
    copies = [
        pltpu.make_async_copy(source, target, sems.at[i])
        for i, (source, target) in enumerate((
            (grad_streams, grad_streams_hbm), (grad_filter, grad_filter_hbm), (mixed, mixed_hbm),
        ))
    ]
    for copy in copies:
        copy.start()
    for copy in copies:
        copy.wait()


def local(projected, short_taps, long_filter, grad_mixed):
    first, second, back, last, twist = (jnp.asarray(table) for table in tables())
    operands = (long_filter, projected, short_taps, grad_mixed, first, second, twist, back, last)
    tokens, channels = grad_mixed.shape
    in_vmem = pl.BlockSpec(memory_space=pltpu.VMEM)
    in_hbm = pl.BlockSpec(memory_space=pltpu.MemorySpace.HBM)
    buffer = pltpu.VMEM((3, DEVICES, SUB * BLOCKS, SIDE), BF16)
    scales = pltpu.VMEM((6, DEVICES, 1, SIDE), F32)
    whole = pltpu.VMEM((DEVICES, SUB * BLOCKS, SIDE), F32)
    out_shape = (
        jax.ShapeDtypeStruct((tokens, channels), BF16),
        jax.ShapeDtypeStruct((3, tokens, channels), BF16),
        jax.ShapeDtypeStruct((tokens, channels), F32),
    )
    results = pl.pallas_call(
        kernel,
        out_shape=out_shape,
        in_specs=[in_hbm] * len(operands),
        out_specs=(in_vmem,) * 3,
        scratch_shapes=[pltpu.VMEM(operand.shape, operand.dtype) for operand in operands]
        + [
            buffer, buffer, buffer, buffer, scales, scales,
            pltpu.VMEM((tokens, channels), F32), whole, whole,
            pltpu.VMEM((3, tokens, channels), F32),
            pltpu.VMEM((3, 16, channels), BF16),
            pltpu.VMEM((3, SUB // GROUP, GROUP * SIDE, 2 * SIDE), F32),
            pltpu.SemaphoreType.DMA((len(operands),)),
            pltpu.SemaphoreType.DMA((12,)),
            pltpu.SemaphoreType.DMA((12,)),
            pltpu.SemaphoreType.DMA((2,)),
        ],
        compiler_params=pltpu.CompilerParams(
            collective_id=0, has_side_effects=True, vmem_limit_bytes=40 * 1024 * 1024
        ),
    )(*[pltpu.with_memory_space_constraint(operand, pltpu.MemorySpace.HBM) for operand in operands])
    return pl.pallas_call(
        write_out,
        out_shape=out_shape,
        in_specs=[in_vmem] * 3,
        out_specs=(in_hbm,) * 3,
        scratch_shapes=[pltpu.SemaphoreType.DMA((3,))],
    )(*[pltpu.with_memory_space_constraint(result, pltpu.VMEM) for result in results])


def solution(mesh):
    in_specs = (P(None, "ctx", "ch"), P(None, None, "ch"), P("ctx", "ch"), P("ctx", "ch"))
    out_specs = (P("ctx", "ch"), P(None, "ctx", "ch"), P("ctx", "ch"))
    return jax.shard_map(local, mesh=mesh, in_specs=in_specs, out_specs=out_specs, check_vma=False)
```

```python
import math

import jax
import jax.numpy as jnp
import ml_dtypes
import numpy as np
from jax import lax
from jax.experimental import pallas as pl
from jax.experimental.pallas import tpu as pltpu
from jax.sharding import PartitionSpec as P

MESH = pl.DeviceIdType.MESH
SIDE = 128
DEVICES = 16
SUB = 8
GROUP = 4
BLOCKS = 8
OFFSET = 1.0 / 64.0
F32, BF16 = jnp.float32, jnp.bfloat16


def halves(table):
    high = table.astype(ml_dtypes.bfloat16)
    low = (table - high.astype(np.float64)).astype(ml_dtypes.bfloat16)
    return high, low


def along(table, axis):
    high, low = halves(table)
    return np.concatenate([high, high, low], axis=axis)


def tables():
    index = np.arange(SIDE)
    outer = 2.0 * math.pi * ((4 * index[:, None] + 1) * index[None, :] % (4 * SIDE)) / (4 * SIDE)
    inner = 2.0 * math.pi * (index[:, None] * index[None, :] % SIDE) / SIDE
    turn = 2.0 * math.pi * ((4 * index[:, None] + 1) * index[None, :]) / (4 * SIDE * SIDE)
    first = np.concatenate([np.cos(outer), -np.sin(outer)], axis=0)
    cos, sin = np.cos(inner), np.sin(inner)
    second = np.block([[cos, -sin], [sin, cos]])
    back = np.block([[cos, sin], [-sin, cos]])
    last = np.concatenate([np.cos(outer).T, -np.sin(outer).T], axis=1) / (SIDE * SIDE)
    twist = np.stack([np.cos(turn), np.sin(turn)]).astype(np.float32)
    return along(first, 1), along(second, 0), along(back, 0), along(last, 1), twist


def split(value):
    high = value.astype(BF16)
    return high, (value - high.astype(F32)).astype(BF16)


def dot(left, right):
    return jnp.dot(left, right, preferred_element_type=F32)


def left_product(table, value):
    high, low = split(value)
    return dot(table[...], jnp.concatenate([high, low, high], axis=0))


def right_product(value, table):
    high, low = split(value)
    return dot(jnp.concatenate([high, low, high], axis=1), table[...])


def scale_of(largest):
    return 8.0 / jnp.maximum(largest, 1e-30)


def coded(value, scale):
    base = jnp.abs(value) * scale + 8.0 * OFFSET
    two = base * base
    four = two * two
    eight = four * four
    sixteen = eight * eight
    power = sixteen * sixteen * eight
    return jnp.where(value < 0.0, -power, power)


def decoded(code, largest):
    root = jnp.exp2(jnp.log2(jnp.abs(code)) * (1.0 / 40.0))
    size = root * (largest * 0.125) - largest * OFFSET
    return jnp.where(code < 0.0, -size, size)


def kernel(
    filt_hbm, proj_hbm, taps_hbm, grad_hbm, first_hbm, second_hbm, twist_hbm, back_hbm, last_hbm,
    mixed, grad_streams, grad_filter,
    filt, proj, taps, grad, first, second, twist, back, last,
    sent, got, made, home, scales_out, scales_in, plain, plain_back, gathered, results, streams, halo, spectra,
    load_sem, send_sem, recv_sem, halo_sem,
):
    loads = [
        pltpu.make_async_copy(source, target, load_sem.at[i])
        for i, (source, target) in enumerate((
            (filt_hbm, filt), (proj_hbm, proj), (taps_hbm, taps), (grad_hbm, grad), (first_hbm, first),
            (second_hbm, second), (twist_hbm, twist), (back_hbm, back), (last_hbm, last),
        ))
    ]
    for load in loads:
        load.start()
    me = lax.axis_index("ctx")
    row, column = me // 4, me % 4

    def peer_of(step):
        return (row + step // 4) % 4 * 4 + (column + step % 4) % 4

    def hops(step):
        return min(step // 4, 4 - step // 4) + min(step % 4, 4 - step % 4)

    peers = [peer_of(step) for step in sorted(range(1, DEVICES), key=hops, reverse=True)]

    def each_peer(action):
        for peer in peers:
            action(peer)

    pairs = [(sent.at[m], got.at[m]) for m in range(3)] + [(made.at[m], home.at[m]) for m in range(3)]
    pairs += [(scales_out.at[m], scales_in.at[m]) for m in range(6)]

    def copy_to(message, peer):
        source, target = pairs[message]
        return pltpu.make_async_remote_copy(
            src_ref=source.at[peer], dst_ref=target.at[me],
            send_sem=send_sem.at[message], recv_sem=recv_sem.at[message],
            device_id={"ctx": peer}, device_id_type=MESH,
        )

    def all_copies(message):
        source, target = pairs[message]
        every = pl.ds(0, DEVICES - 1)
        return pltpu.make_async_remote_copy(
            src_ref=source.at[every], dst_ref=target.at[every],
            send_sem=send_sem.at[message], recv_sem=recv_sem.at[message],
            device_id={"ctx": peers[0]}, device_id_type=MESH,
        )

    def send(message):
        def start(peer):
            copy_to(message + 6, peer).start()
            copy_to(message, peer).start()
        each_peer(start)
        for source, target in (pairs[message], pairs[message + 6]):
            target[me] = source[me]

    def receive(message):
        all_copies(message + 6).wait_recv()
        all_copies(message).wait_recv()

    def rows_of(block):
        return pl.ds(pl.multiple_of(block * SIDE, SIDE), SIDE)

    def code_rows(pair):
        return pl.ds(pl.multiple_of(pair * 2 * SUB, 2 * SUB), 2 * SUB)

    def turned_out(message, source):
        largest = jnp.max(jnp.abs(source[...]), axis=0, keepdims=True)
        scales_out[message] = jnp.broadcast_to(largest[None], (DEVICES, 1, SIDE))
        scale = scale_of(largest)

        def body(pair, carry):
            turned = [
                coded(source[rows_of(2 * pair + i), :], scale).T.reshape(DEVICES, SUB, SIDE) for i in range(2)
            ]
            sent[message, :, code_rows(pair), :] = jnp.concatenate(turned, axis=1).astype(BF16)
            return carry
        lax.fori_loop(0, BLOCKS // 2, body, 0)

    barrier = pltpu.get_barrier_semaphore()
    each_peer(lambda peer: pl.semaphore_signal(barrier, inc=1, device_id={"ctx": peer}, device_id_type=MESH))
    loads[0].wait()
    turned_out(0, filt)
    pl.semaphore_wait(barrier, DEVICES - 1)
    loads[1].wait()
    after, before = (me + 1) % DEVICES, (me + DEVICES - 1) % DEVICES
    tail = pl.ds(BLOCKS * SIDE - 16, 16)

    def halo_copy(peer):
        return pltpu.make_async_remote_copy(
            src_ref=proj.at[:, tail, :], dst_ref=halo, send_sem=halo_sem.at[0], recv_sem=halo_sem.at[1],
            device_id={"ctx": peer}, device_id_type=MESH,
        )

    halo_copy(after).start()
    send(0)

    def short(stream, block, previous):
        now = proj[stream, rows_of(block), :].astype(F32)
        window = jnp.concatenate([previous[8:], now], axis=0)
        value = (
            taps[stream, 0:1, :] * now
            + taps[stream, 1:2, :] * window[7 : 7 + SIDE]
            + taps[stream, 2:3, :] * window[6 : 6 + SIDE]
        )
        streams[stream, rows_of(block), :] = value
        return value

    def inside(stream, block):
        return proj[stream, pl.ds(pl.multiple_of(block * SIDE - 16, 16), 16), :].astype(F32)

    def edge(stream):
        return jnp.where(me > 0, halo[stream].astype(F32), 0.0)

    def key_value(block, previous):
        plain[rows_of(block), :] = short(1, block, previous(1)) * short(2, block, previous(2))

    def back_gated(block, previous):
        plain_back[rows_of(block), :] = short(0, block, previous(0)) * grad[rows_of(block), :].astype(F32)

    def later_blocks(make):
        def body(block, carry):
            make(block, lambda stream: inside(stream, block))
            return carry
        lax.fori_loop(1, BLOCKS, body, 0)

    loads[2].wait()
    later_blocks(key_value)
    loads[3].wait()
    later_blocks(back_gated)
    halo_copy(before).wait_recv()
    key_value(0, edge)
    turned_out(1, plain)
    send(1)
    back_gated(0, edge)
    turned_out(2, plain_back)
    send(2)

    def lane_is_own(shape, axis):
        lane = lax.broadcasted_iota(jnp.int32, shape, len(shape) - 1)
        return lane == SUB * me + lax.broadcasted_iota(jnp.int32, shape, axis)

    def gather(message):
        receive(message)
        shape = (DEVICES, SUB, SIDE)
        rows = jnp.broadcast_to(scales_in[message], shape)
        largest = jnp.sum(jnp.where(lane_is_own(shape, 1), rows, 0.0), axis=2, keepdims=True)
        for source in range(DEVICES):
            code = got[message, source].astype(F32).reshape(BLOCKS, SUB, SIDE)
            gathered[source] = decoded(code, largest[source : source + 1]).reshape(BLOCKS * SUB, SIDE)

    def scatter(message):
        for target in range(DEVICES):
            value = results[target].reshape(BLOCKS, SUB, SIDE)
            largest = jnp.max(jnp.max(jnp.abs(value), axis=0), axis=1, keepdims=True)
            spread = jnp.where(lane_is_own((SUB, SIDE), 0), largest, 0.0)
            scales_out[message, target] = jnp.sum(spread, axis=0, keepdims=True)
            made[message - 3, target] = coded(value, scale_of(largest)[None]).reshape(BLOCKS * SUB, SIDE).astype(BF16)
        send(message)

    def forward(pair):
        parts = [gathered[:, pl.ds(GROUP * pair + i, SUB, stride=SUB), :].reshape(SIDE, SIDE) for i in range(GROUP)]
        mixed_rows = left_product(first, jnp.concatenate(parts, axis=1))
        cos, sin = twist[0], twist[1]
        rows = []
        for i in range(GROUP):
            real = mixed_rows[:SIDE, i * SIDE : (i + 1) * SIDE]
            imag = mixed_rows[SIDE:, i * SIDE : (i + 1) * SIDE]
            rows.append(jnp.concatenate([real * cos + imag * sin, imag * cos - real * sin], axis=1))
        return right_product(jnp.concatenate(rows, axis=0), second)

    def inverse(pair, real, imag):
        value = right_product(jnp.concatenate([real, imag], axis=1), back)
        cos, sin = twist[0], twist[1]
        columns = []
        for i in range(GROUP):
            real = value[i * SIDE : (i + 1) * SIDE, :SIDE]
            imag = value[i * SIDE : (i + 1) * SIDE, SIDE:]
            columns.append(jnp.concatenate([real * cos - imag * sin, real * sin + imag * cos], axis=0))
        result = left_product(last, jnp.concatenate(columns, axis=1))
        for i in range(GROUP):
            results[:, pl.ds(GROUP * pair + i, SUB, stride=SUB), :] = result[:, i * SIDE : (i + 1) * SIDE].reshape(
                DEVICES, SUB, SIDE
            )

    def parts_of(value):
        return value[:, :SIDE], value[:, SIDE:]

    def each_pair(action):
        for pair in range(SUB // GROUP):
            action(pair)

    def spectrum(signal):
        def action(pair):
            spectra[signal, pair] = forward(pair)
        each_pair(action)

    def conv_pair(pair):
        (fr, fi), (vr, vi) = parts_of(spectra[0, pair]), parts_of(spectra[1, pair])
        inverse(pair, fr * vr - fi * vi, fr * vi + fi * vr)

    def stream_pair(pair):
        (fr, fi), (br, bi) = parts_of(spectra[0, pair]), parts_of(spectra[2, pair])
        inverse(pair, fr * br + fi * bi, fr * bi - fi * br)

    def filt_pair(pair):
        (vr, vi), (br, bi) = parts_of(spectra[1, pair]), parts_of(spectra[2, pair])
        inverse(pair, vr * br + vi * bi, vr * bi - vi * br)

    for load in loads[4:]:
        load.wait()
    gather(0)
    spectrum(0)
    gather(1)
    spectrum(1)
    each_pair(conv_pair)
    scatter(3)
    gather(2)
    spectrum(2)
    each_pair(stream_pair)
    scatter(4)
    each_pair(filt_pair)
    scatter(5)

    def turned_home(message, action):
        receive(message)
        largest = jnp.sum(scales_in[message], axis=0)

        def body(pair, carry):
            code = home[message - 3, :, code_rows(pair), :].astype(F32)
            for i in range(2):
                turned = code[:, i * SUB : (i + 1) * SUB, :].reshape(SIDE, SIDE).T
                action(rows_of(2 * pair + i), decoded(turned, largest))
            return carry
        lax.fori_loop(0, BLOCKS // 2, body, 0)

    def conv_home(rows, value):
        mixed[rows, :] = (streams[0, rows, :] * value).astype(BF16)
        grad_streams[0, rows, :] = (grad[rows, :].astype(F32) * value).astype(BF16)

    def stream_home(rows, value):
        grad_streams[1, rows, :] = (value * streams[2, rows, :]).astype(BF16)
        grad_streams[2, rows, :] = (value * streams[1, rows, :]).astype(BF16)

    def filt_home(rows, value):
        grad_filter[rows, :] = value * (1.0 / SIDE)

    turned_home(3, conv_home)
    turned_home(4, stream_home)
    for message in (0, 1, 2, 3, 4, 6, 7, 8, 9, 10):
        all_copies(message).wait_send()
    halo_copy(after).wait_send()
    turned_home(5, filt_home)
    for message in (5, 11):
        all_copies(message).wait_send()


def write_out(mixed, grad_streams, grad_filter, mixed_hbm, grad_streams_hbm, grad_filter_hbm, sems):
    copies = [
        pltpu.make_async_copy(source, target, sems.at[i])
        for i, (source, target) in enumerate((
            (grad_streams, grad_streams_hbm), (grad_filter, grad_filter_hbm), (mixed, mixed_hbm),
        ))
    ]
    for copy in copies:
        copy.start()
    for copy in copies:
        copy.wait()


def local(projected, short_taps, long_filter, grad_mixed):
    first, second, back, last, twist = (jnp.asarray(table) for table in tables())
    operands = (long_filter, projected, short_taps, grad_mixed, first, second, twist, back, last)
    tokens, channels = grad_mixed.shape
    in_vmem = pl.BlockSpec(memory_space=pltpu.VMEM)
    in_hbm = pl.BlockSpec(memory_space=pltpu.MemorySpace.HBM)
    buffer = pltpu.VMEM((3, DEVICES, SUB * BLOCKS, SIDE), BF16)
    scales = pltpu.VMEM((6, DEVICES, 1, SIDE), F32)
    whole = pltpu.VMEM((DEVICES, SUB * BLOCKS, SIDE), F32)
    out_shape = (
        jax.ShapeDtypeStruct((tokens, channels), BF16),
        jax.ShapeDtypeStruct((3, tokens, channels), BF16),
        jax.ShapeDtypeStruct((tokens, channels), F32),
    )
    results = pl.pallas_call(
        kernel,
        out_shape=out_shape,
        in_specs=[in_hbm] * len(operands),
        out_specs=(in_vmem,) * 3,
        scratch_shapes=[pltpu.VMEM(operand.shape, operand.dtype) for operand in operands]
        + [
            buffer, buffer, buffer, buffer, scales, scales,
            pltpu.VMEM((tokens, channels), F32), pltpu.VMEM((tokens, channels), F32), whole, whole,
            pltpu.VMEM((3, tokens, channels), F32),
            pltpu.VMEM((3, 16, channels), BF16),
            pltpu.VMEM((3, SUB // GROUP, GROUP * SIDE, 2 * SIDE), F32),
            pltpu.SemaphoreType.DMA((len(operands),)),
            pltpu.SemaphoreType.DMA((12,)),
            pltpu.SemaphoreType.DMA((12,)),
            pltpu.SemaphoreType.DMA((2,)),
        ],
        compiler_params=pltpu.CompilerParams(
            collective_id=0, has_side_effects=True, vmem_limit_bytes=40 * 1024 * 1024
        ),
    )(*[pltpu.with_memory_space_constraint(operand, pltpu.MemorySpace.HBM) for operand in operands])
    return pl.pallas_call(
        write_out,
        out_shape=out_shape,
        in_specs=[in_vmem] * 3,
        out_specs=(in_hbm,) * 3,
        scratch_shapes=[pltpu.SemaphoreType.DMA((3,))],
    )(*[pltpu.with_memory_space_constraint(result, pltpu.VMEM) for result in results])


def solution(mesh):
    in_specs = (P(None, "ctx", "ch"), P(None, None, "ch"), P("ctx", "ch"), P("ctx", "ch"))
    out_specs = (P("ctx", "ch"), P(None, "ctx", "ch"), P("ctx", "ch"))
    return jax.shard_map(local, mesh=mesh, in_specs=in_specs, out_specs=out_specs, check_vma=False)
```
